256 devices in a mesh: depth: 8 (over z), imgy: 8 (over y, core), imgx: 4 (over x).
Axes of the slice: x: 4, y: 4, z: 8, core: 2. Of those that a mesh axis runs over, the one named last changes fastest.
Arguments:
- coefficients: float32 [512, 512, 512], P('depth', 'imgy', 'imgx'), may hold values from -6 to 6
- shifts: int32 [2, 512], P(None, 'depth'), may hold values from -63 to 63, as said below
- fraction: float32 [2, 512], P(None, 'depth'), may hold values from 0 to 1
- absorb: float32 [512], P('depth'), may hold values from 0.3 to 3
Outputs:
- image: float32 [4, 8, 64, 512], P(None, 'imgy', 'depth', 'imgx')
The draws below stay inside these ranges and needn't reach their ends.
Inputs may be any that keep to these rules, and one draw needn't show every extreme that they name: `shifts`: each of the two rows is non-decreasing along the slices; slice 0 has the smallest value and slice 512 - 1 the largest.
All inputs are finite; a program needn't handle non-finite values.
Results may differ from the reference program's by a relative error of at most 0.0003.
Values sent between devices are 32-bit elements; how exact they have to be, the bound alone decides.
No kernel may reach another device: no remote copies, remote signals or barrier semaphores. Data moves between devices by JAX's collectives and lax.ppermute only.
A program may use at most 128 MiB of HBM per device.

```python
import math
import jax
import jax.numpy as jnp
from jax import lax

BRICK = 64
LEVELS = 3
NZ = 512
NY = 512
NX = 512
N_IMGY = 8


def monotone_offsets(key):
    steps_up = jax.random.randint(key, (NZ,), 0, 2)
    position = lax.broadcasted_iota(jnp.int32, (NZ,), 0)
    steps_up = jnp.where(position == 0, 0, jnp.where(position == NZ - 1, 1, steps_up))
    climbed = jnp.cumsum(steps_up)
    return climbed * (2 * (BRICK - 1)) // climbed[-1] - (BRICK - 1)


def draw_shifts(key, part):
    first_row = monotone_offsets(jax.random.fold_in(key, 11))
    second_row = monotone_offsets(jax.random.fold_in(key, 23))
    return jnp.stack([first_row, second_row], axis=0).astype(jnp.int32)


def level_of(own_key, dims, cuts, least, top_value):
    level, own = 1.0, jax.random.fold_in(own_key, 6)
    for dim, blocks in cuts:
        draws = jnp.exp(jax.random.uniform(jax.random.fold_in(own, dim), (blocks,), jnp.float32, least / len(cuts), top_value / len(cuts)))
        level = level * jnp.repeat(draws, dims[dim] // blocks).reshape([-1 if axis == dim else 1 for axis in range(len(dims))])
    return level


def bell_draw(rng, extent, width, bound, shards=(), dtype=jnp.bfloat16):
    drawn = jax.random.normal(rng, extent, jnp.float32) * width
    if len(shards) > 0:
        drawn = level_of(rng, extent, shards, -0.22, 0.18) * drawn
    return jnp.clip(drawn, min=-bound, max=bound).astype(dtype)


def setup_inputs(seed: int = 0) -> dict:
    key_list = jax.random.split(jax.random.key(seed), 5)
    return {
        "coefficients": bell_draw(key_list[0], (NZ, NY, NX), 1.0, 6.0, ((0, 8), (1, 8), (2, 4)), jnp.float32),
        "shifts": draw_shifts(jax.random.fold_in(key_list[4], 71), 0),
        "fraction": jnp.clip(1.0 * jax.random.uniform(key_list[2], (2, NZ), jnp.float32) ** level_of(key_list[2], (2, NZ), ((1, 8),), -0.2, 0.2), 0.0, 1.0),
        "absorb": jnp.clip(jnp.exp(math.log(3.0) - 2.3025851 * jax.random.uniform(key_list[3], (NZ,), jnp.float32) ** level_of(key_list[3], (NZ,), ((0, 8),), -0.2, 0.2)), 0.3, 3.0),
    }


def inverse_step(cube_block, dimension, half_span):
    low_part = lax.slice_in_dim(cube_block, 0, half_span, axis=dimension)
    high_part = lax.slice_in_dim(cube_block, half_span, 2 * half_span, axis=dimension)
    even_cells = low_part - 0.5 * high_part
    odd_cells = even_cells + high_part
    joined = jnp.stack([even_cells, odd_cells], axis=dimension + 1)
    return joined.reshape(cube_block.shape)


def inverse_haar(volume):
    for level_index in reversed(range(LEVELS)):
        half_span = BRICK >> (level_index + 1)
        corner = (slice(None), slice(0, 2 * half_span), slice(None), slice(0, 2 * half_span), slice(None), slice(0, 2 * half_span))
        cube_block = volume[corner]
        for dimension in (1, 3, 5):
            cube_block = inverse_step(cube_block, dimension, half_span)
        volume = volume.at[corner].set(cube_block)
    return volume


def palette(sheared):
    return jnp.stack([jax.nn.sigmoid(1.5 * sheared), jnp.exp(-0.5 * sheared * sheared), jax.nn.sigmoid(0.8 - sheared)], axis=0)


def shear(window, frac_y, frac_x):
    upper = (1.0 - frac_x) * window[..., 1:, 1:] + frac_x * window[..., 1:, :-1]
    lower = (1.0 - frac_x) * window[..., :-1, 1:] + frac_x * window[..., :-1, :-1]
    return (1.0 - frac_y) * upper + frac_y * lower


def reference(coefficients, shifts, fraction, absorb):
    depth_cells, row_cells, col_cells = coefficients.shape
    volume = coefficients.reshape(depth_cells // BRICK, BRICK, row_cells // BRICK, BRICK, col_cells // BRICK, BRICK)
    volume = inverse_haar(volume).reshape(depth_cells, row_cells, col_cells)
    padded = jnp.pad(volume, ((0, 0), (BRICK, BRICK), (BRICK, BRICK)))
    scale_factor = 2.0 / depth_cells

    def advance(running, slice_items):
        total_depth, radiance = running
        plane, offset_y, offset_x, frac_y, frac_x, absorb_rate = slice_items
        start_y = (BRICK - offset_y - 1).astype(jnp.int32)
        start_x = (BRICK - offset_x - 1).astype(jnp.int32)
        window = lax.dynamic_slice(plane, (start_y, start_x), (row_cells + 1, col_cells + 1))
        sheared = shear(window, frac_y, frac_x)
        optical = absorb_rate * scale_factor * jax.nn.softplus(sheared)
        emission = (1.0 - jnp.exp(-optical))[None] * palette(sheared)
        radiance = radiance + jnp.exp(-total_depth)[None] * emission
        return (total_depth + optical, radiance), None

    start_state = (jnp.zeros((row_cells, col_cells), jnp.float32), jnp.zeros((3, row_cells, col_cells), jnp.float32))
    (thickness, radiance), _ = lax.scan(advance, start_state, (padded, shifts[0], shifts[1], fraction[0], fraction[1], absorb))
    image = jnp.concatenate([radiance, (1.0 - jnp.exp(-thickness))[None]], axis=0)
    return image.reshape(4, N_IMGY, row_cells // N_IMGY, col_cells)
```

```python
import functools
import math

import jax
import jax.numpy as jnp
from jax import lax
from jax.experimental import pallas as pl
from jax.experimental.pallas import tpu as pltpu
from jax.sharding import PartitionSpec as P

BRICK = 64
SLAB = 64
ROWS = 64
COLS = 128
STRIDE = 80
HEAD = 8
BLOCKS = 24
LN2 = math.log(2.0)
TINT0 = (0.5, 1.0, 1.0 / (1.0 + math.exp(-0.8)))
VMEM_SPEC = pl.BlockSpec(memory_space=pltpu.VMEM)
SMEM_SPEC = pl.BlockSpec(memory_space=pltpu.SMEM)
INTERPRET = False


def call(kernel, out_shape, in_specs, scratch=(), flops=1000, bytes_moved=1000):
    specs = jax.tree.map(lambda _: VMEM_SPEC, out_shape)
    return pl.pallas_call(
        kernel,
        out_shape=out_shape,
        in_specs=in_specs,
        out_specs=specs,
        scratch_shapes=list(scratch),
        interpret=INTERPRET,
        cost_estimate=pl.CostEstimate(flops=flops, bytes_accessed=bytes_moved, transcendentals=0),
    )


def f32(*shape):
    return jax.ShapeDtypeStruct(shape, jnp.float32)


def lane_table(half):
    source = lax.broadcasted_iota(jnp.int32, (2 * COLS, COLS), 0) % COLS
    target = lax.broadcasted_iota(jnp.int32, (2 * COLS, COLS), 1)
    local = target % BRICK
    start = target - local
    pair = local // 2
    weight = jnp.where(local % 2 == 1, 0.5, -0.5)
    inside = local < 2 * half
    low = jnp.where(inside & (source == start + pair), 1.0, 0.0)
    high = jnp.where(inside & (source == start + half + pair), weight, 0.0)
    return (low + high).astype(jnp.bfloat16)


def lane_lift(block, table):
    coarse = block.astype(jnp.bfloat16)
    rest = (block - coarse.astype(jnp.float32)).astype(jnp.bfloat16)
    both = jnp.concatenate([coarse, rest], axis=1)
    return jnp.dot(both, table, preferred_element_type=jnp.float32)


def lift_kernel(c_ref, d_ref, row_ref, col_ref, s2_ref, s1_ref, plane_ref):
    lane = lax.broadcasted_iota(jnp.int32, (1, COLS), 1)

    def level(half, below, out_ref, on_result, init, unroll):
        table = lane_table(half)

        def step(i, carry):
            if below is None:
                low = c_ref[i, : 2 * half, :]
            else:
                corner = jnp.where(lane % BRICK < half, below[i], c_ref[i, :half, :])
                low = jnp.concatenate([corner, c_ref[i, half : 2 * half, :]], axis=0)
            high = c_ref[i + half, : 2 * half, :]
            planes = []
            even = low - 0.5 * high
            for part in (even, even + high):
                row_even = part[:half] - 0.5 * part[half:]
                planes += [row_even, row_even + part[half:]]
            result = lane_lift(jnp.concatenate(planes, axis=0), table)
            for odd in range(2):
                for row_odd in range(2):
                    start = (2 * odd + row_odd) * half
                    out_ref[2 * i + odd, pl.ds(row_odd, half, stride=2), :] = result[start : start + half]
            return on_result(i, result, carry)

        return lax.fori_loop(0, half, step, init, unroll=unroll)

    def ignore(i, result, carry):
        return carry

    def boundary(i, result, plane):
        for odd in range(2):
            z = 2 * i + odd
            piece = result[64 * odd : 64 * odd + 64]
            row_ref[pl.ds(z, 1), :] = piece[63:64]
            plane = jnp.where(lane == z, pltpu.roll(piece, z + 1, 1), plane)
        return plane

    level(8, None, s2_ref, ignore, 0, 2)
    level(16, s2_ref, s1_ref, ignore, 0, 2)
    plane = level(32, s1_ref, d_ref, boundary, jnp.zeros((64, COLS), jnp.float32), 2)
    plane_ref[...] = plane
    for row_odd in range(2):
        col_ref[pl.ds(row_odd, 32, stride=2), :] = plane_ref[pl.ds(32 * row_odd, 32), :]
    row_ref[pl.ds(64, 8), :] = jnp.broadcast_to(plane[63:64], (8, COLS))


def optics(sheared, rate):
    size = jnp.abs(sheared)
    fall = jnp.exp(-size)
    tail = jnp.where(fall < 1e-3, fall * (1.0 - 0.5 * fall), jnp.log(1.0 + fall))
    return (
        rate * (jnp.maximum(sheared, 0.0) + tail),
        0.5 + 0.5 * jnp.tanh(0.75 * sheared),
        jnp.exp(-0.5 * sheared * sheared),
        0.5 + 0.5 * jnp.tanh(0.4 - 0.5 * sheared),
    )


def shade_kernel(
    scale, shift_ref, frac_ref, absorb_ref, span_ref, edge_ref, d_ref, halo_row_ref, halo_col_ref, corner_ref, last_ref,
    fvec_ref, up_ref, own_ref, down_ref, g_ref, v_ref, hu_ref,
):
    lane = lax.broadcasted_iota(jnp.int32, (8, COLS), 1)
    sub = lax.broadcasted_iota(jnp.int32, (8, COLS), 0)
    last_row = edge_ref[0] == 1
    last_col = edge_ref[1] == 1
    zero = jnp.zeros((8, COLS), jnp.float32)
    fy_lanes = fvec_ref[0:1, :]
    fx_lanes = fvec_ref[1:2, :]
    rate_lanes = fvec_ref[2:3, :] * scale

    for part in range(4):
        g_ref[part, pl.ds(0, 8), :] = zero
        v_ref[part, pl.ds(0, 8), :] = zero
        v_ref[part, pl.ds(80, 8), :] = zero

    for t in range(9):
        for which, plane, above in ((0, halo_col_ref, corner_ref[7:8, :]), (1, last_ref, halo_row_ref[64:65, :])):
            here = plane[8 * t : 8 * t + 8, :] if t < 8 else zero
            before = above if t == 0 else plane[8 * t - 1 : 8 * t, :]
            behind = jnp.where(sub == 0, before, pltpu.roll(here, 1, 0))
            mixed = here + fy_lanes * (behind - here)
            if which == 0:
                hu_ref[pl.ds(8 * t, 8), :] = mixed
            else:
                values = optics(fx_lanes * mixed, rate_lanes)
                for part in range(4):
                    value = values[part]
                    if t == 8:
                        value = jnp.where((sub == 0) & last_row, value, 0.0)
                    v_ref[part, pl.ds(8 + 8 * t, 8), :] = value

    def slice_step(z, carry):
        fy, fx, rate = frac_ref[0, z], frac_ref[1, z], absorb_ref[z] * scale
        k = shift_ref[1, z] + 64
        base = HEAD + STRIDE * z
        for t in range(9):
            if t == 0:
                here = d_ref[z, 0:8, :]
                behind = jnp.where(sub == 0, halo_row_ref[pl.ds(z, 1), :], pltpu.roll(here, 1, 0))
            elif t == 8:
                here = zero
                behind = jnp.where(sub == 0, d_ref[z, 63:64, :], 0.0)
            else:
                here = d_ref[z, 8 * t : 8 * t + 8, :]
                behind = d_ref[z, 8 * t - 1 : 8 * t + 7, :]
            mixed = here + fy * (behind - here)
            left = jnp.where(lane == 0, pltpu.roll(hu_ref[pl.ds(8 * t, 8), :], COLS - z, 1), pltpu.roll(mixed, 1, 1))
            sheared = pltpu.roll(mixed + fx * (left - mixed), k, 1)
            values = optics(sheared, rate)
            for part in range(4):
                value = values[part]
                if t == 8:
                    value = jnp.where((sub == 0) & last_row, value, 0.0)
                g_ref[part, pl.ds(pl.multiple_of(base + 8 * t, 8), 8), :] = value
        for part in range(4):
            g_ref[part, pl.ds(pl.multiple_of(base + 72, 8), 8), :] = zero
        return carry

    lax.fori_loop(0, SLAB, slice_step, 0, unroll=2)

    def composite(edge):
        for out, out_ref in enumerate((up_ref, own_ref, down_ref)):

            def block_step(block, carry):
                index = 8 * out + block

                def ray_step(group, state):
                    for offset in range(4):
                        z = 4 * group + offset
                        low = 8 * index - 64 - shift_ref[0, z]
                        valid = (low >= -7) & (low <= 64)
                        low = jnp.where(valid, low, 72)
                        k = shift_ref[1, z] + 64
                        row = HEAD + STRIDE * z + low
                        values = [g_ref[part, pl.ds(row, 8), :] for part in range(4)]
                        right = lane < k
                        left_values = [jnp.where(right, 0.0, values[0])] + values[1:]
                        right_values = [jnp.where(right, values[0], 0.0)] + values[1:]
                        if edge:
                            for part in range(4):
                                extra = v_ref[part, pl.ds(8 + low, 8), :]
                                extra = pltpu.roll(extra, (k - z + COLS) % COLS, 1)
                                right_values[part] = jnp.where(lane == k, extra, right_values[part])
                        new_state = []
                        for half, (optical, *tints) in enumerate((left_values, right_values)):
                            depth, through, *sums = state[half]
                            depth = depth + optical
                            after = jnp.exp(-depth)
                            weight = through - after
                            sums = [total + weight * tint for total, tint in zip(sums, tints)]
                            new_state.append((depth, after, *sums))
                        state = tuple(new_state)
                    return state

                start = (zero, zero + 1.0, zero, zero, zero)
                state = lax.fori_loop(span_ref[0, index], span_ref[1, index], ray_step, (start, start))
                rows = pl.ds(pl.multiple_of(8 * block, 8), 8)
                for half in range(2):
                    depth, _, *sums = state[half]
                    for channel in range(3):
                        out_ref[half, channel, rows, :] = sums[channel]
                    out_ref[half, 3, rows, :] = depth
                return carry

            lax.fori_loop(0, 8, block_step, 0)

    pl.when(last_col)(lambda: composite(True))
    pl.when(jnp.logical_not(last_col))(lambda: composite(False))


def over(front, behind):
    through = jnp.exp(-front[3])
    return [front[c] + through * behind[c] for c in range(3)] + [front[3] + behind[3]]


def channels(ref, *index):
    return [ref[(*index, c)] for c in range(4)]


def rows_kernel(own_ref, below_ref, above_ref, mine_ref, left_ref, right_ref):
    lane = lax.broadcasted_iota(jnp.int32, (1, COLS), 1)
    halves = []
    for half in range(2):
        merged = over(channels(own_ref, half), channels(above_ref, half))
        halves.append(over(channels(below_ref, half), merged))
    for c in range(4):
        low, high = halves[0][c], halves[1][c]
        low_turned, high_turned = pltpu.roll(low, 64, 1), pltpu.roll(high, 64, 1)
        mine_ref[c] = jnp.where(lane < 64, low_turned, high_turned)
        left_ref[c] = jnp.where(lane < 64, low[:32], low_turned[32:])
        right_ref[c] = jnp.where(lane < 64, high_turned[:32], high[32:])


def columns_kernel(scale, edge_ref, mine_ref, own_right_ref, from_right_ref, from_left_ref, zrow_ref, zcol_ref, out_ref):
    lane = lax.broadcasted_iota(jnp.int32, (1, COLS), 1)
    last_col = edge_ref[1] == 1

    def unpack(packed):
        turned = pltpu.roll(packed, 64, 1)
        return turned, packed

    front, behind, mine = [], [], []
    for c in range(4):
        piece = from_right_ref[c]
        turned = pltpu.roll(piece, 64, 1)
        upper = jnp.concatenate([turned, piece], axis=0)
        piece = from_left_ref[c]
        turned = pltpu.roll(piece, 64, 1)
        lower = jnp.concatenate([piece, turned], axis=0)
        own = mine_ref[c]
        front.append(jnp.where(lane < 64, own, upper))
        behind.append(jnp.where(lane < 64, lower, own))
    inner = over(front, behind)
    pre = jnp.maximum(zrow_ref[:, 0:1], zcol_ref[0:1, :])
    post = jnp.minimum(jnp.maximum(zrow_ref[:, 1:2], zcol_ref[1:2, :]), zcol_ref[2:3, :] - pre)
    post = jnp.maximum(post, 0.0)
    flat = []
    for amount in (pre, post):
        depth = (scale * LN2) * amount
        fade = 1.0 - jnp.exp(-depth)
        flat.append([TINT0[c] * fade for c in range(3)] + [depth])
    whole = over(flat[0], over(inner, flat[1]))
    pieces = out_ref.shape[0]
    height = ROWS // pieces
    for p in range(pieces):
        for c in range(4):
            out_ref[p, c] = whole[c][p * height : (p + 1) * height]


def fold_kernel(in_ref, out_ref):
    merged = channels(in_ref, 0)
    for slab in range(1, in_ref.shape[0]):
        merged = over(merged, channels(in_ref, slab))
    for c in range(3):
        out_ref[c] = merged[c]
    out_ref[3] = 1.0 - jnp.exp(-merged[3])


def body(coefficients, shifts, fraction, absorb):
    depth_count = lax.axis_size("depth")
    row_count = lax.axis_size("imgy")
    col_count = lax.axis_size("imgx")
    scale = 2.0 / (SLAB * depth_count)
    iy, ix = lax.axis_index("imgy"), lax.axis_index("imgx")

    volume, row_plane, col_plane = call(
        lift_kernel,
        (f32(SLAB, ROWS, COLS), f32(72, COLS), f32(ROWS, COLS)),
        [VMEM_SPEC],
        [
            pltpu.VMEM((16, 16, COLS), jnp.float32),
            pltpu.VMEM((32, 32, COLS), jnp.float32),
            pltpu.VMEM((64, COLS), jnp.float32),
        ],
        flops=300_000_000,
        bytes_moved=4 << 20,
    )(coefficients)

    row_up = [(i, i + 1) for i in range(row_count - 1)]
    row_down = [(i + 1, i) for i in range(row_count - 1)]
    col_up = [(i, i + 1) for i in range(col_count - 1)]
    col_down = [(i + 1, i) for i in range(col_count - 1)]
    both_up = [
        (y * col_count + x, (y + 1) * col_count + x + 1) for y in range(row_count - 1) for x in range(col_count - 1)
    ]
    halo_row = lax.ppermute(row_plane, "imgy", row_up)
    halo_col = lax.ppermute(col_plane, "imgx", col_up)
    corner = lax.ppermute(col_plane[56:64], ("imgy", "imgx"), both_up)

    shift_rows, shift_cols = shifts[0], shifts[1]
    starts = 8 * jnp.arange(BLOCKS, dtype=jnp.int32)
    first = jnp.sum(shift_rows[None, :] < starts[:, None] - 128, axis=1, dtype=jnp.int32)
    end = jnp.sum(shift_rows[None, :] <= starts[:, None] - 57, axis=1, dtype=jnp.int32)
    span = jnp.stack([first // 4, (end + 3) // 4])
    edge = jnp.stack([iy == row_count - 1, ix == col_count - 1]).astype(jnp.int32)
    vectors = jnp.pad(jnp.concatenate([fraction, absorb[None]], axis=0), ((0, 5), (0, COLS - SLAB)))

    sent = f32(2, 4, ROWS, COLS)
    up, own, down = call(
        functools.partial(shade_kernel, scale),
        (sent, sent, sent),
        [SMEM_SPEC] * 5 + [VMEM_SPEC] * 6,
        [
            pltpu.VMEM((4, HEAD + SLAB * STRIDE, COLS), jnp.float32),
            pltpu.VMEM((4, 88, COLS), jnp.float32),
            pltpu.VMEM((72, COLS), jnp.float32),
        ],
        flops=300_000_000,
        bytes_moved=4 << 20,
    )(shifts, fraction, absorb, span, edge, volume, halo_row, halo_col, corner, col_plane, vectors)

    below = lax.ppermute(up, "imgy", row_down)
    above = lax.ppermute(down, "imgy", row_up)
    packed = f32(4, ROWS // 2, COLS)
    mine, left, right = call(rows_kernel, (f32(4, ROWS, COLS), packed, packed), [VMEM_SPEC] * 3)(own, below, above)
    from_right = lax.ppermute(left, "imgx", col_down)
    from_left = lax.ppermute(right, "imgx", col_up)

    image_rows = iy * ROWS + jnp.arange(ROWS, dtype=jnp.int32)
    image_cols = ix * COLS + jnp.arange(COLS, dtype=jnp.int32)

    def outside(pixels, offsets, limit):
        position = pixels[:, None] - offsets[None, :]
        pre = jnp.sum(jnp.where(position > limit, absorb[None, :], 0.0), axis=1)
        post = jnp.sum(jnp.where(position < 0, absorb[None, :], 0.0), axis=1)
        return pre, post

    zrow = jnp.stack(outside(image_rows, shift_rows, ROWS * row_count), axis=1)
    zcol = jnp.stack(
        [*outside(image_cols, shift_cols, COLS * col_count), jnp.broadcast_to(jnp.sum(absorb), (COLS,))], axis=0
    )
    pieces = call(
        functools.partial(columns_kernel, scale),
        f32(depth_count, 4, ROWS // depth_count, COLS),
        [SMEM_SPEC] + [VMEM_SPEC] * 6,
    )(edge, mine, right, from_right, from_left, zrow, zcol)
    incoming = lax.all_to_all(pieces, "depth", split_axis=0, concat_axis=0, tiled=True)
    image = call(fold_kernel, f32(4, ROWS // depth_count, COLS), [VMEM_SPEC])(incoming)
    return image[:, None]


def solution(mesh):
    in_specs = (P("depth", "imgy", "imgx"), P(None, "depth"), P(None, "depth"), P("depth"))
    out_specs = P(None, "imgy", "depth", "imgx")
    return jax.shard_map(body, mesh=mesh, in_specs=in_specs, out_specs=out_specs, check_vma=False)
```

```python
import functools
import math

import jax
import jax.numpy as jnp
from jax import lax
from jax.experimental import pallas as pl
from jax.experimental.pallas import tpu as pltpu
from jax.sharding import PartitionSpec as P

BRICK = 64
SLAB = 64
ROWS = 64
COLS = 128
EXT = 208
LN2 = math.log(2.0)
VMEM_SPEC = pl.BlockSpec(memory_space=pltpu.VMEM)
SMEM_SPEC = pl.BlockSpec(memory_space=pltpu.SMEM)
INTERPRET = False


def call(kernel, out_shape, in_specs, scratch=(), flops=1000, bytes_moved=1000):
    specs = jax.tree.map(lambda _: VMEM_SPEC, out_shape)
    return pl.pallas_call(
        kernel,
        out_shape=out_shape,
        in_specs=in_specs,
        out_specs=specs,
        scratch_shapes=list(scratch),
        interpret=INTERPRET,
        compiler_params=pltpu.CompilerParams(vmem_limit_bytes=24 << 20),
        cost_estimate=pl.CostEstimate(flops=flops, bytes_accessed=bytes_moved, transcendentals=0),
    )


def f32(*shape):
    return jax.ShapeDtypeStruct(shape, jnp.float32)


def lane_table(half):
    source = lax.broadcasted_iota(jnp.int32, (2 * COLS, COLS), 0) % COLS
    target = lax.broadcasted_iota(jnp.int32, (2 * COLS, COLS), 1)
    local = target % BRICK
    start = target - local
    pair = local // 2
    weight = jnp.where(local % 2 == 1, 0.5, -0.5)
    inside = local < 2 * half
    low = jnp.where(inside & (source == start + pair), 1.0, 0.0)
    high = jnp.where(inside & (source == start + half + pair), weight, 0.0)
    return (low + high).astype(jnp.bfloat16)


def lane_lift(block, table):
    coarse = block.astype(jnp.bfloat16)
    rest = (block - coarse.astype(jnp.float32)).astype(jnp.bfloat16)
    both = jnp.concatenate([coarse, rest], axis=1)
    return jnp.dot(both, table, preferred_element_type=jnp.float32)


def lift_kernel(c_ref, d_ref, row_ref, col_ref, s2_ref, s1_ref, plane_ref):
    lane = lax.broadcasted_iota(jnp.int32, (1, COLS), 1)

    def level(half, below, out_ref, on_result, init, unroll):
        table = lane_table(half)

        def step(i, carry):
            if below is None:
                low = c_ref[i, : 2 * half, :]
            else:
                corner = jnp.where(lane % BRICK < half, below[i], c_ref[i, :half, :])
                low = jnp.concatenate([corner, c_ref[i, half : 2 * half, :]], axis=0)
            high = c_ref[i + half, : 2 * half, :]
            planes = []
            even = low - 0.5 * high
            for part in (even, even + high):
                row_even = part[:half] - 0.5 * part[half:]
                planes += [row_even, row_even + part[half:]]
            result = lane_lift(jnp.concatenate(planes, axis=0), table)
            for odd in range(2):
                for row_odd in range(2):
                    start = (2 * odd + row_odd) * half
                    out_ref[2 * i + odd, pl.ds(row_odd, half, stride=2), :] = result[start : start + half]
            return on_result(i, result, carry)

        return lax.fori_loop(0, half, step, init, unroll=unroll)

    def ignore(i, result, carry):
        return carry

    def boundary(i, result, plane):
        for odd in range(2):
            z = 2 * i + odd
            piece = result[64 * odd : 64 * odd + 64]
            row_ref[pl.ds(z, 1), :] = piece[63:64]
            plane = jnp.where(lane == z, pltpu.roll(piece, z + 1, 1), plane)
        return plane

    level(8, None, s2_ref, ignore, 0, 2)
    level(16, s2_ref, s1_ref, ignore, 0, 2)
    plane = level(32, s1_ref, d_ref, boundary, jnp.zeros((64, COLS), jnp.float32), 2)
    plane_ref[...] = plane
    for row_odd in range(2):
        col_ref[pl.ds(row_odd, 32, stride=2), :] = plane_ref[pl.ds(32 * row_odd, 32), :]
    row_ref[pl.ds(64, 8), :] = jnp.broadcast_to(plane[63:64], (8, COLS))


def optics(sheared, rate):
    soft = jnp.maximum(sheared, 0.0) + jnp.log(1.0 + jnp.exp(-jnp.abs(sheared)))
    return (
        jnp.tanh(0.75 * sheared),
        jnp.exp(-0.5 * (sheared * sheared)),
        jnp.tanh(0.4 - 0.5 * sheared),
        jnp.exp(-rate * soft),
    )


def absorb_sample(acc_ref, half, rows, tints, keep):
    through = acc_ref[4 * half + 3, rows, :]
    after = through * keep
    weight = through - after
    acc_ref[4 * half + 3, rows, :] = after
    for channel in range(3):
        acc_ref[4 * half + channel, rows, :] += weight * tints[channel]


def shade_kernel(
    scale, shift_ref, frac_ref, absorb_ref, edge_ref, d_ref, halo_row_ref, halo_col_ref, corner_ref, last_ref,
    fvec_ref, up_ref, own_ref, down_ref, acc_ref, v_ref, hu_ref,
):
    lane = lax.broadcasted_iota(jnp.int32, (8, COLS), 1)
    sub = lax.broadcasted_iota(jnp.int32, (8, COLS), 0)
    first_lane = lane == 0
    last_row = edge_ref[0] == 1
    last_col = edge_ref[1] == 1
    zero = jnp.zeros((8, COLS), jnp.float32)
    fy_lanes = fvec_ref[0:1, :]
    fx_lanes = fvec_ref[1:2, :]
    rate_lanes = fvec_ref[2:3, :] * scale

    for index in range(8):
        acc_ref[index] = jnp.full((EXT, COLS), 1.0 if index % 4 == 3 else 0.0, jnp.float32)

    def lerp_plane(plane, above, t):
        here = plane[8 * t : 8 * t + 8, :] if t < 8 else zero
        before = above if t == 0 else plane[8 * t - 1 : 8 * t, :]
        behind = jnp.where(sub == 0, before, pltpu.roll(here, 1, 0))
        return here + fy_lanes * (behind - here)

    for t in range(9):
        hu_ref[pl.ds(8 * t, 8), :] = lerp_plane(halo_col_ref, corner_ref[7:8, :], t)

    def sheared_tile(z, t, fy, fx, k):
        if t == 0:
            here = d_ref[z, 0:8, :]
            behind = jnp.where(sub == 0, halo_row_ref[pl.ds(z, 1), :], pltpu.roll(here, 1, 0))
        elif t == 8:
            here = zero
            behind = jnp.where(sub == 0, d_ref[z, 63:64, :], 0.0)
        else:
            here = d_ref[z, 8 * t : 8 * t + 8, :]
            behind = d_ref[z, 8 * t - 1 : 8 * t + 7, :]
        mixed = here + fy * (behind - here)
        left = jnp.where(first_lane, pltpu.roll(hu_ref[pl.ds(8 * t, 8), :], COLS - z, 1), pltpu.roll(mixed, 1, 1))
        return pltpu.roll(mixed + fx * (left - mixed), k, 1)

    def shade_tile(z, t, fy, fx, k, rate, right):
        *tints, keep = optics(sheared_tile(z, t, fy, fx, k), rate)
        if t == 8:
            keep = jnp.where(sub == 0, keep, 1.0)
        rows = pl.ds(shift_ref[0, z] + 64 + 8 * t, 8)
        absorb_sample(acc_ref, 0, rows, tints, jnp.where(right, 1.0, keep))
        absorb_sample(acc_ref, 1, rows, tints, jnp.where(right, keep, 1.0))

    def slice_scalars(z):
        k = shift_ref[1, z] + 64
        return frac_ref[0, z], frac_ref[1, z], k, absorb_ref[z] * scale, lane < k

    @pl.when(last_col)
    def _():
        for t in range(9):
            *tints, keep = optics(fx_lanes * lerp_plane(last_ref, halo_row_ref[64:65, :], t), rate_lanes)
            if t == 8:
                keep = jnp.where((sub == 0) & last_row, keep, 1.0)
            for part, value in enumerate((*tints, keep)):
                v_ref[part, pl.ds(8 * t, 8), :] = value

        def column_step(group):
            for offset in range(2):
                z = 2 * group + offset
                k = shift_ref[1, z] + 64
                at = lane == k
                for t in range(9):
                    values = [
                        pltpu.roll(v_ref[part, pl.ds(8 * t, 8), :], (k - z + COLS) % COLS, 1) for part in range(4)
                    ]
                    rows = pl.ds(shift_ref[0, z] + 64 + 8 * t, 8)
                    absorb_sample(acc_ref, 1, rows, values[:3], jnp.where(at, values[3], 1.0))
            return group + 1

        lax.while_loop(
            lambda group: (group < SLAB // 2) & (shift_ref[1, jnp.minimum(2 * group, SLAB - 1)] < 0), column_step, 0
        )

    @pl.when(last_row)
    def _():
        def row_step(group):
            for offset in range(4):
                z = 4 * group + offset
                fy, fx, k, rate, right = slice_scalars(z)
                shade_tile(z, 8, fy, fx, k, rate, right)
            return group + 1

        lax.while_loop(
            lambda group: (group < SLAB // 4) & (shift_ref[0, jnp.minimum(4 * group, SLAB - 1)] < 0), row_step, 0
        )

    def slice_step(z, carry):
        fy, fx, k, rate, right = slice_scalars(z)
        for t in range(8):
            shade_tile(z, t, fy, fx, k, rate, right)
        return carry

    lax.fori_loop(0, SLAB, slice_step, 0, unroll=2)

    for out, out_ref in enumerate((up_ref, own_ref, down_ref)):
        for half in range(2):
            for channel in range(4):
                value = acc_ref[4 * half + channel, pl.ds(64 * out, 64), :]
                out_ref[half, channel] = 1.0 - value if channel == 3 else value


def over(front, behind):
    through = 1.0 - front[3]
    return [front[c] + through * behind[c] for c in range(4)]


def channels(ref, *index):
    return [ref[(*index, c)] for c in range(4)]


def rows_kernel(own_ref, below_ref, above_ref, mine_ref, left_ref, right_ref):
    lane = lax.broadcasted_iota(jnp.int32, (1, COLS), 1)
    halves = []
    for half in range(2):
        merged = over(channels(own_ref, half), channels(above_ref, half))
        halves.append(over(channels(below_ref, half), merged))
    for c in range(4):
        low, high = halves[0][c], halves[1][c]
        low_turned, high_turned = pltpu.roll(low, 64, 1), pltpu.roll(high, 64, 1)
        mine_ref[c] = jnp.where(lane < 64, low_turned, high_turned)
        left_ref[c] = jnp.where(lane < 64, low[:32], low_turned[32:])
        right_ref[c] = jnp.where(lane < 64, high_turned[:32], high[32:])


def columns_kernel(scale, mine_ref, from_right_ref, from_left_ref, zrow_ref, zcol_ref, out_ref):
    lane = lax.broadcasted_iota(jnp.int32, (1, COLS), 1)
    front, behind = [], []
    for c in range(4):
        piece = from_right_ref[c]
        upper = jnp.concatenate([pltpu.roll(piece, 64, 1), piece], axis=0)
        piece = from_left_ref[c]
        lower = jnp.concatenate([piece, pltpu.roll(piece, 64, 1)], axis=0)
        own = mine_ref[c]
        front.append(jnp.where(lane < 64, own, upper))
        behind.append(jnp.where(lane < 64, lower, own))
    inner = over(front, behind)
    pre = jnp.maximum(zrow_ref[:, 0:1], zcol_ref[0:1, :])
    post = jnp.minimum(jnp.maximum(zrow_ref[:, 1:2], zcol_ref[1:2, :]), zcol_ref[2:3, :] - pre)
    flat = []
    for amount in (pre, jnp.maximum(post, 0.0)):
        fade = 1.0 - jnp.exp((-scale * LN2) * amount)
        flat.append([jnp.zeros_like(fade), fade, math.tanh(0.4) * fade, fade])
    whole = over(flat[0], over(inner, flat[1]))
    pieces = out_ref.shape[0]
    height = ROWS // pieces
    for p in range(pieces):
        for c in range(4):
            out_ref[p, c] = whole[c][p * height : (p + 1) * height]


def fold_kernel(in_ref, out_ref):
    merged = channels(in_ref, 0)
    for slab in range(1, in_ref.shape[0]):
        merged = over(merged, channels(in_ref, slab))
    out_ref[0] = 0.5 * (merged[3] + merged[0])
    out_ref[1] = merged[1]
    out_ref[2] = 0.5 * (merged[3] + merged[2])
    out_ref[3] = merged[3]


def body(coefficients, shifts, fraction, absorb):
    depth_count = lax.axis_size("depth")
    row_count = lax.axis_size("imgy")
    col_count = lax.axis_size("imgx")
    scale = 2.0 / (SLAB * depth_count)
    iy, ix = lax.axis_index("imgy"), lax.axis_index("imgx")

    volume, row_plane, col_plane = call(
        lift_kernel,
        (f32(SLAB, ROWS, COLS), f32(72, COLS), f32(ROWS, COLS)),
        [VMEM_SPEC],
        [
            pltpu.VMEM((16, 16, COLS), jnp.float32),
            pltpu.VMEM((32, 32, COLS), jnp.float32),
            pltpu.VMEM((64, COLS), jnp.float32),
        ],
        flops=300_000_000,
        bytes_moved=4 << 20,
    )(coefficients)

    row_up = [(i, i + 1) for i in range(row_count - 1)]
    row_down = [(i + 1, i) for i in range(row_count - 1)]
    col_up = [(i, i + 1) for i in range(col_count - 1)]
    col_down = [(i + 1, i) for i in range(col_count - 1)]
    both_up = [
        (y * col_count + x, (y + 1) * col_count + x + 1) for y in range(row_count - 1) for x in range(col_count - 1)
    ]
    halo_row = lax.ppermute(row_plane, "imgy", row_up)
    halo_col = lax.ppermute(col_plane, "imgx", col_up)
    corner = lax.ppermute(col_plane[56:64], ("imgy", "imgx"), both_up)

    shift_rows, shift_cols = shifts[0], shifts[1]
    edge = jnp.stack([iy == row_count - 1, ix == col_count - 1]).astype(jnp.int32)
    vectors = jnp.pad(jnp.concatenate([fraction, absorb[None]], axis=0), ((0, 5), (0, COLS - SLAB)))

    sent = f32(2, 4, ROWS, COLS)
    up, own, down = call(
        functools.partial(shade_kernel, scale),
        (sent, sent, sent),
        [SMEM_SPEC] * 4 + [VMEM_SPEC] * 6,
        [
            pltpu.VMEM((8, EXT, COLS), jnp.float32),
            pltpu.VMEM((4, 72, COLS), jnp.float32),
            pltpu.VMEM((72, COLS), jnp.float32),
        ],
        flops=300_000_000,
        bytes_moved=4 << 20,
    )(shifts, fraction, absorb, edge, volume, halo_row, halo_col, corner, col_plane, vectors)

    below = lax.ppermute(up, "imgy", row_down)
    above = lax.ppermute(down, "imgy", row_up)
    packed = f32(4, ROWS // 2, COLS)
    mine, left, right = call(rows_kernel, (f32(4, ROWS, COLS), packed, packed), [VMEM_SPEC] * 3)(own, below, above)
    from_right = lax.ppermute(left, "imgx", col_down)
    from_left = lax.ppermute(right, "imgx", col_up)

    image_rows = iy * ROWS + jnp.arange(ROWS, dtype=jnp.int32)
    image_cols = ix * COLS + jnp.arange(COLS, dtype=jnp.int32)

    def outside(pixels, offsets, limit):
        position = pixels[:, None] - offsets[None, :]
        pre = jnp.sum(jnp.where(position > limit, absorb[None, :], 0.0), axis=1)
        post = jnp.sum(jnp.where(position < 0, absorb[None, :], 0.0), axis=1)
        return pre, post

    zrow = jnp.stack(outside(image_rows, shift_rows, ROWS * row_count), axis=1)
    zcol = jnp.stack(
        [*outside(image_cols, shift_cols, COLS * col_count), jnp.broadcast_to(jnp.sum(absorb), (COLS,))], axis=0
    )
    pieces = call(
        functools.partial(columns_kernel, scale),
        f32(depth_count, 4, ROWS // depth_count, COLS),
        [VMEM_SPEC] * 5,
    )(mine, from_right, from_left, zrow, zcol)
    incoming = lax.all_to_all(pieces, "depth", split_axis=0, concat_axis=0, tiled=True)
    image = call(fold_kernel, f32(4, ROWS // depth_count, COLS), [VMEM_SPEC])(incoming)
    return image[:, None]


def solution(mesh):
    in_specs = (P("depth", "imgy", "imgx"), P(None, "depth"), P(None, "depth"), P("depth"))
    out_specs = P(None, "imgy", "depth", "imgx")
    return jax.shard_map(body, mesh=mesh, in_specs=in_specs, out_specs=out_specs, check_vma=False)
```

```python
import functools
import math

import jax
import jax.numpy as jnp
from jax import lax
from jax.experimental import pallas as pl
from jax.experimental.pallas import tpu as pltpu
from jax.sharding import PartitionSpec as P

BRICK = 64
SLAB = 64
ROWS = 64
COLS = 128
EXT = 208
SLICE_UNROLL = 8
ROW_UNROLL = 16
COLUMN_UNROLL = 8
LN2 = math.log(2.0)
VMEM_SPEC = pl.BlockSpec(memory_space=pltpu.VMEM)
SMEM_SPEC = pl.BlockSpec(memory_space=pltpu.SMEM)
INTERPRET = False


def call(kernel, out_shape, in_specs, scratch=(), flops=1000, bytes_moved=1000):
    specs = jax.tree.map(lambda _: VMEM_SPEC, out_shape)
    return pl.pallas_call(
        kernel,
        out_shape=out_shape,
        in_specs=in_specs,
        out_specs=specs,
        scratch_shapes=list(scratch),
        interpret=INTERPRET,
        compiler_params=pltpu.CompilerParams(vmem_limit_bytes=24 << 20),
        cost_estimate=pl.CostEstimate(flops=flops, bytes_accessed=bytes_moved, transcendentals=0),
    )


def f32(*shape):
    return jax.ShapeDtypeStruct(shape, jnp.float32)


def lane_table(half):
    source = lax.broadcasted_iota(jnp.int32, (2 * COLS, COLS), 0) % COLS
    target = lax.broadcasted_iota(jnp.int32, (2 * COLS, COLS), 1)
    local = target % BRICK
    start = target - local
    pair = local // 2
    weight = jnp.where(local % 2 == 1, 0.5, -0.5)
    inside = local < 2 * half
    low = jnp.where(inside & (source == start + pair), 1.0, 0.0)
    high = jnp.where(inside & (source == start + half + pair), weight, 0.0)
    return (low + high).astype(jnp.bfloat16)


def lane_lift(block, table):
    coarse = block.astype(jnp.bfloat16)
    rest = (block - coarse.astype(jnp.float32)).astype(jnp.bfloat16)
    both = jnp.concatenate([coarse, rest], axis=1)
    return jnp.dot(both, table, preferred_element_type=jnp.float32)


def lift_kernel(c_ref, d_ref, row_ref, col_ref, s2_ref, s1_ref, plane_ref):
    lane = lax.broadcasted_iota(jnp.int32, (1, COLS), 1)

    def level(half, below, out_ref, on_result, init, unroll):
        table = lane_table(half)

        def step(i, carry):
            if below is None:
                low = c_ref[i, : 2 * half, :]
            else:
                corner = jnp.where(lane % BRICK < half, below[i], c_ref[i, :half, :])
                low = jnp.concatenate([corner, c_ref[i, half : 2 * half, :]], axis=0)
            high = c_ref[i + half, : 2 * half, :]
            planes = []
            even = low - 0.5 * high
            for part in (even, even + high):
                row_even = part[:half] - 0.5 * part[half:]
                planes += [row_even, row_even + part[half:]]
            result = lane_lift(jnp.concatenate(planes, axis=0), table)
            for odd in range(2):
                for row_odd in range(2):
                    start = (2 * odd + row_odd) * half
                    out_ref[2 * i + odd, pl.ds(row_odd, half, stride=2), :] = result[start : start + half]
            return on_result(i, result, carry)

        return lax.fori_loop(0, half, step, init, unroll=unroll)

    def ignore(i, result, carry):
        return carry

    def boundary(i, result, plane):
        for odd in range(2):
            z = 2 * i + odd
            piece = result[64 * odd : 64 * odd + 64]
            row_ref[pl.ds(z, 1), :] = piece[63:64]
            plane = jnp.where(lane == z, pltpu.roll(piece, z + 1, 1), plane)
        return plane

    level(8, None, s2_ref, ignore, 0, 8)
    level(16, s2_ref, s1_ref, ignore, 0, 16)
    plane = level(32, s1_ref, d_ref, boundary, jnp.zeros((64, COLS), jnp.float32), 16)
    plane_ref[...] = plane
    for row_odd in range(2):
        col_ref[pl.ds(row_odd, 32, stride=2), :] = plane_ref[pl.ds(32 * row_odd, 32), :]
    row_ref[pl.ds(64, 8), :] = jnp.broadcast_to(plane[63:64], (8, COLS))


def optics(sheared, rate):
    soft = jnp.maximum(sheared, 0.0) + jnp.log(1.0 + jnp.exp(-jnp.abs(sheared)))
    return (
        jnp.tanh(0.75 * sheared),
        jnp.exp(-0.5 * (sheared * sheared)),
        jnp.tanh(0.4 - 0.5 * sheared),
        jnp.exp(-rate * soft),
    )


def absorb_sample(view, half, tints, keep):
    through = view[4 * half + 3]
    after = through * keep
    weight = through - after
    view[4 * half + 3] = after
    for channel in range(3):
        view[4 * half + channel] = view[4 * half + channel] + weight * tints[channel]


def shade_kernel(
    scale, shift_ref, frac_ref, absorb_ref, edge_ref, d_ref, halo_row_ref, halo_col_ref, corner_ref, last_ref,
    fvec_ref, near_ref, own_ref, far_ref, acc_ref, v_ref, hu_ref,
):
    lane = lax.broadcasted_iota(jnp.int32, (1, COLS), 1)
    sub = lax.broadcasted_iota(jnp.int32, (8, COLS), 0)
    last_row = edge_ref[0] == 1
    last_col = edge_ref[1] == 1
    zero = jnp.zeros((8, COLS), jnp.float32)
    fy_lanes = fvec_ref[0:1, :]
    fx_lanes = fvec_ref[1:2, :]
    rate_lanes = fvec_ref[2:3, :] * scale

    for index in range(8):
        acc_ref[index] = jnp.full((EXT, COLS), 1.0 if index % 4 == 3 else 0.0, jnp.float32)

    def lerp_plane(plane, above):
        first = jnp.where(sub == 0, above, pltpu.roll(plane[0:8, :], 1, 0))
        here = jnp.concatenate([plane[...], zero], axis=0)
        behind = jnp.concatenate([first, plane[7:63, :], jnp.where(sub == 0, plane[63:64, :], 0.0)], axis=0)
        return here + fy_lanes * (behind - here)

    hu_ref[...] = lerp_plane(halo_col_ref, corner_ref[7:8, :])

    def window(z, first_row, rows):
        return acc_ref.at[:, pl.ds(shift_ref[0, z] + 64 + first_row, rows), :]

    def shade(z, here, behind, halo, first_row, mask=None):
        k = shift_ref[1, z] + 64
        right = lane < k
        mixed = here + frac_ref[0, z] * (behind - here)
        left = jnp.where(lane == 0, pltpu.roll(halo, COLS - z, 1), pltpu.roll(mixed, 1, 1))
        sheared = pltpu.roll(mixed + frac_ref[1, z] * (left - mixed), k, 1)
        *tints, keep = optics(sheared, absorb_ref[z] * scale)
        if mask is not None:
            keep = jnp.where(mask, keep, 1.0)
        view = window(z, first_row, here.shape[0])
        absorb_sample(view, 0, tints, jnp.where(right, 1.0, keep))
        absorb_sample(view, 1, tints, jnp.where(right, keep, 1.0))

    @pl.when(last_col)
    def _():
        *tints, keep = optics(fx_lanes * lerp_plane(last_ref, halo_row_ref[64:65, :]), rate_lanes)
        row = lax.broadcasted_iota(jnp.int32, (72, COLS), 0)
        keep = jnp.where((row < 64) | ((row == 64) & last_row), keep, 1.0)
        for part, value in enumerate((*tints, keep)):
            v_ref[part] = value

        def column_step(group):
            for offset in range(COLUMN_UNROLL):
                z = COLUMN_UNROLL * group + offset
                k = shift_ref[1, z] + 64
                *tints, keep = [pltpu.roll(v_ref[part], (k - z + COLS) % COLS, 1) for part in range(4)]
                absorb_sample(window(z, 0, 72), 1, tints, jnp.where(lane == k, keep, 1.0))
            return group + 1

        lax.while_loop(
            lambda group: (group < SLAB // COLUMN_UNROLL)
            & (shift_ref[1, jnp.minimum(COLUMN_UNROLL * group, SLAB - 1)] < 0),
            column_step,
            0,
        )

    @pl.when(last_row)
    def _():
        def row_step(group):
            for offset in range(ROW_UNROLL):
                z = ROW_UNROLL * group + offset
                behind = jnp.where(sub == 0, d_ref[z, 63:64, :], 0.0)
                shade(z, zero, behind, hu_ref[64:72, :], 64, sub == 0)
            return group + 1

        lax.while_loop(
            lambda group: (group < SLAB // ROW_UNROLL)
            & (shift_ref[0, jnp.minimum(ROW_UNROLL * group, SLAB - 1)] < 0),
            row_step,
            0,
        )

    def slice_step(z, carry):
        first = jnp.where(sub == 0, halo_row_ref[pl.ds(z, 1), :], pltpu.roll(d_ref[z, 0:8, :], 1, 0))
        behind = jnp.concatenate([first, d_ref[z, 7:63, :]], axis=0)
        shade(z, d_ref[z], behind, hu_ref[0:64, :], 0)
        return carry

    lax.fori_loop(0, SLAB, slice_step, 0, unroll=SLICE_UNROLL)

    odd = edge_ref[2]
    for start, out_ref in ((128 - 128 * odd, near_ref), (64, own_ref), (128 * odd, far_ref)):
        for half in range(2):
            for channel in range(4):
                value = acc_ref[4 * half + channel, pl.ds(pl.multiple_of(start, 64), 64), :]
                out_ref[half, channel] = 1.0 - value if channel == 3 else value


def over(front, behind):
    through = 1.0 - front[3]
    return [front[c] + through * behind[c] for c in range(4)]


def channels(ref, *index):
    return [ref[(*index, c)] for c in range(4)]


def rows_kernel(edge_ref, own_ref, near_ref, far_ref, mine_ref, near_out_ref, far_out_ref):
    lane = lax.broadcasted_iota(jnp.int32, (1, COLS), 1)
    odd_row, odd_col = edge_ref[2] == 1, edge_ref[3] == 1
    halves = []
    for half in range(2):
        near, far = channels(near_ref, half), channels(far_ref, half)
        below = [jnp.where(odd_row, f, n) for n, f in zip(near, far)]
        above = [jnp.where(odd_row, n, f) for n, f in zip(near, far)]
        halves.append(over(below, over(channels(own_ref, half), above)))
    for c in range(4):
        low, high = halves[0][c], halves[1][c]
        low_turned, high_turned = pltpu.roll(low, 64, 1), pltpu.roll(high, 64, 1)
        mine_ref[c] = jnp.where(lane < 64, low_turned, high_turned)
        left = jnp.where(lane < 64, low[:32], low_turned[32:])
        right = jnp.where(lane < 64, high_turned[:32], high[32:])
        near_out_ref[c] = jnp.where(odd_col, left, right)
        far_out_ref[c] = jnp.where(odd_col, right, left)


def columns_kernel(scale, edge_ref, mine_ref, near_ref, far_ref, zrow_ref, zcol_ref, fvec_ref, out_ref):
    lane = lax.broadcasted_iota(jnp.int32, (1, COLS), 1)
    odd_col = edge_ref[3] == 1
    front, behind = [], []
    for c in range(4):
        near, far = near_ref[c], far_ref[c]
        piece = jnp.where(odd_col, far, near)
        upper = jnp.concatenate([pltpu.roll(piece, 64, 1), piece], axis=0)
        piece = jnp.where(odd_col, near, far)
        lower = jnp.concatenate([piece, pltpu.roll(piece, 64, 1)], axis=0)
        own = mine_ref[c]
        front.append(jnp.where(lane < 64, own, upper))
        behind.append(jnp.where(lane < 64, lower, own))
    inner = over(front, behind)
    total = jnp.sum(fvec_ref[2:3, :], axis=1, keepdims=True)
    pre = jnp.maximum(zrow_ref[:, 0:1], zcol_ref[0:1, :])
    post = jnp.minimum(jnp.maximum(zrow_ref[:, 1:2], zcol_ref[1:2, :]), total - pre)
    flat = []
    for amount in (pre, jnp.maximum(post, 0.0)):
        fade = 1.0 - jnp.exp((-scale * LN2) * amount)
        flat.append([jnp.zeros_like(fade), fade, math.tanh(0.4) * fade, fade])
    whole = over(flat[0], over(inner, flat[1]))
    pieces = out_ref.shape[0]
    height = ROWS // pieces
    for p in range(pieces):
        for c in range(4):
            out_ref[p, c] = whole[c][p * height : (p + 1) * height]


def fold_kernel(in_ref, out_ref):
    merged = channels(in_ref, 0)
    for slab in range(1, in_ref.shape[0]):
        merged = over(merged, channels(in_ref, slab))
    out_ref[0] = 0.5 * (merged[3] + merged[0])
    out_ref[1] = merged[1]
    out_ref[2] = 0.5 * (merged[3] + merged[2])
    out_ref[3] = merged[3]


def matching(count, first):
    pairs = [(i, i + 1) for i in range(first, count - 1, 2)]
    return pairs + [(j, i) for i, j in pairs]


def body(coefficients, shifts, fraction, absorb):
    depth_count = lax.axis_size("depth")
    row_count = lax.axis_size("imgy")
    col_count = lax.axis_size("imgx")
    scale = 2.0 / (SLAB * depth_count)
    iy, ix = lax.axis_index("imgy"), lax.axis_index("imgx")

    volume, row_plane, col_plane = call(
        lift_kernel,
        (f32(SLAB, ROWS, COLS), f32(72, COLS), f32(ROWS, COLS)),
        [VMEM_SPEC],
        [
            pltpu.VMEM((16, 16, COLS), jnp.float32),
            pltpu.VMEM((32, 32, COLS), jnp.float32),
            pltpu.VMEM((64, COLS), jnp.float32),
        ],
        flops=300_000_000,
        bytes_moved=4 << 20,
    )(coefficients)

    row_up = [(i, i + 1) for i in range(row_count - 1)]
    col_up = [(i, i + 1) for i in range(col_count - 1)]
    both_up = [
        (y * col_count + x, (y + 1) * col_count + x + 1) for y in range(row_count - 1) for x in range(col_count - 1)
    ]
    halo_row = lax.ppermute(row_plane, "imgy", row_up)
    halo_col = lax.ppermute(col_plane, "imgx", col_up)
    corner = lax.ppermute(col_plane[56:64], ("imgy", "imgx"), both_up)

    shift_rows, shift_cols = shifts[0], shifts[1]
    edge = jnp.stack([iy == row_count - 1, ix == col_count - 1, iy % 2 == 1, ix % 2 == 1]).astype(jnp.int32)
    vectors = jnp.pad(jnp.concatenate([fraction, absorb[None]], axis=0), ((0, 5), (0, COLS - SLAB)))

    sent = f32(2, 4, ROWS, COLS)
    near, own, far = call(
        functools.partial(shade_kernel, scale),
        (sent, sent, sent),
        [SMEM_SPEC] * 4 + [VMEM_SPEC] * 6,
        [
            pltpu.VMEM((8, EXT, COLS), jnp.float32),
            pltpu.VMEM((4, 72, COLS), jnp.float32),
            pltpu.VMEM((72, COLS), jnp.float32),
        ],
        flops=300_000_000,
        bytes_moved=4 << 20,
    )(shifts, fraction, absorb, edge, volume, halo_row, halo_col, corner, col_plane, vectors)

    near = lax.ppermute(near, "imgy", matching(row_count, 0))
    far = lax.ppermute(far, "imgy", matching(row_count, 1))
    packed = f32(4, ROWS // 2, COLS)
    mine, near, far = call(rows_kernel, (f32(4, ROWS, COLS), packed, packed), [SMEM_SPEC] + [VMEM_SPEC] * 3)(
        edge, own, near, far
    )
    near = lax.ppermute(near, "imgx", matching(col_count, 0))
    far = lax.ppermute(far, "imgx", matching(col_count, 1))

    image_rows = iy * ROWS + jnp.arange(ROWS, dtype=jnp.int32)
    image_cols = ix * COLS + jnp.arange(COLS, dtype=jnp.int32)

    def outside(pixels, offsets, limit):
        position = pixels[:, None] - offsets[None, :]
        pre = jnp.sum(jnp.where(position > limit, absorb[None, :], 0.0), axis=1)
        post = jnp.sum(jnp.where(position < 0, absorb[None, :], 0.0), axis=1)
        return pre, post

    zrow = jnp.stack(outside(image_rows, shift_rows, ROWS * row_count), axis=1)
    zcol = jnp.stack(outside(image_cols, shift_cols, COLS * col_count), axis=0)
    pieces = call(
        functools.partial(columns_kernel, scale),
        f32(depth_count, 4, ROWS // depth_count, COLS),
        [SMEM_SPEC] + [VMEM_SPEC] * 6,
    )(edge, mine, near, far, zrow, zcol, vectors)
    incoming = lax.all_to_all(pieces, "depth", split_axis=0, concat_axis=0, tiled=True)
    image = call(fold_kernel, f32(4, ROWS // depth_count, COLS), [VMEM_SPEC])(incoming)
    return image[:, None]


def solution(mesh):
    in_specs = (P("depth", "imgy", "imgx"), P(None, "depth"), P(None, "depth"), P("depth"))
    out_specs = P(None, "imgy", "depth", "imgx")
    return jax.shard_map(body, mesh=mesh, in_specs=in_specs, out_specs=out_specs, check_vma=False)
```

```python
import functools
import math

import jax
import jax.numpy as jnp
from jax import lax
from jax.experimental import pallas as pl
from jax.experimental.pallas import tpu as pltpu
from jax.sharding import PartitionSpec as P

BRICK = 64
SLAB = 64
ROWS = 64
COLS = 128
EXT = 208
SLICE_UNROLL = 8
LN2 = math.log(2.0)
VMEM_SPEC = pl.BlockSpec(memory_space=pltpu.VMEM)
SMEM_SPEC = pl.BlockSpec(memory_space=pltpu.SMEM)
INTERPRET = False


def call(kernel, out_shape, in_specs, scratch=(), flops=1000, bytes_moved=1000):
    specs = jax.tree.map(lambda _: VMEM_SPEC, out_shape)
    return pl.pallas_call(
        kernel,
        out_shape=out_shape,
        in_specs=in_specs,
        out_specs=specs,
        scratch_shapes=list(scratch),
        interpret=INTERPRET,
        compiler_params=pltpu.CompilerParams(vmem_limit_bytes=24 << 20),
        cost_estimate=pl.CostEstimate(flops=flops, bytes_accessed=bytes_moved, transcendentals=0),
    )


def f32(*shape):
    return jax.ShapeDtypeStruct(shape, jnp.float32)


def lane_table(half):
    source = lax.broadcasted_iota(jnp.int32, (2 * COLS, COLS), 0) % COLS
    target = lax.broadcasted_iota(jnp.int32, (2 * COLS, COLS), 1)
    local = target % BRICK
    start = target - local
    pair = local // 2
    weight = jnp.where(local % 2 == 1, 0.5, -0.5)
    inside = local < 2 * half
    low = jnp.where(inside & (source == start + pair), 1.0, 0.0)
    high = jnp.where(inside & (source == start + half + pair), weight, 0.0)
    return (low + high).astype(jnp.bfloat16)


def lane_lift(block, table):
    coarse = block.astype(jnp.bfloat16)
    rest = (block - coarse.astype(jnp.float32)).astype(jnp.bfloat16)
    both = jnp.concatenate([coarse, rest], axis=1)
    return jnp.dot(both, table, preferred_element_type=jnp.float32)


def softplus(sheared):
    return jnp.maximum(sheared, 0.0) + jnp.log(1.0 + jnp.exp(-jnp.abs(sheared)))


def tint(sheared):
    return jnp.tanh(0.75 * sheared), jnp.exp(-0.5 * (sheared * sheared)), jnp.tanh(0.4 - 0.5 * sheared)


def absorb_sample(view, half, tints, keep):
    through = view[4 * half + 3]
    after = through * keep
    weight = through - after
    view[4 * half + 3] = after
    for channel in range(3):
        view[4 * half + channel] = view[4 * half + channel] + weight * tints[channel]


def tile_kernel(
    scale, shift_ref, frac_ref, absorb_ref, edge_ref, c_ref, near_ref, own_ref, far_ref, rows_ref, cols_ref,
    s2_ref, s1_ref, d_ref, plane_ref, acc_ref,
):
    lane = lax.broadcasted_iota(jnp.int32, (1, COLS), 1)
    sub = lax.broadcasted_iota(jnp.int32, (8, COLS), 0)

    def level(half, below, out_ref, on_result, init, unroll):
        table = lane_table(half)

        def step(i, carry):
            if below is None:
                low = c_ref[i, : 2 * half, :]
            else:
                corner = jnp.where(lane % BRICK < half, below[i], c_ref[i, :half, :])
                low = jnp.concatenate([corner, c_ref[i, half : 2 * half, :]], axis=0)
            high = c_ref[i + half, : 2 * half, :]
            planes = []
            even = low - 0.5 * high
            for part in (even, even + high):
                row_even = part[:half] - 0.5 * part[half:]
                planes += [row_even, row_even + part[half:]]
            result = lane_lift(jnp.concatenate(planes, axis=0), table)
            for odd in range(2):
                for row_odd in range(2):
                    start = (2 * odd + row_odd) * half
                    out_ref[2 * i + odd, pl.ds(row_odd, half, stride=2), :] = result[start : start + half]
            return on_result(i, result, carry)

        return lax.fori_loop(0, half, step, init, unroll=unroll)

    def ignore(i, result, carry):
        return carry

    def boundary(i, result, plane):
        for odd in range(2):
            z = 2 * i + odd
            piece = result[64 * odd : 64 * odd + 64]
            rows_ref[pl.ds(z, 1), :] = piece[63:64]
            rows_ref[pl.ds(64 + z, 1), :] = piece[0:1]
            plane = jnp.where(lane == z, pltpu.roll(piece, z + 1, 1), plane)
            plane = jnp.where(lane == z + 64, pltpu.roll(piece, z + 64, 1), plane)
        return plane

    level(8, None, s2_ref, ignore, 0, 8)
    level(16, s2_ref, s1_ref, ignore, 0, 16)
    plane_ref[...] = level(32, s1_ref, d_ref, boundary, jnp.zeros((64, COLS), jnp.float32), 16)
    for row_odd in range(2):
        cols_ref[pl.ds(row_odd, 32, stride=2), :] = plane_ref[pl.ds(32 * row_odd, 32), :]

    for index in range(8):
        acc_ref[index] = jnp.full((EXT, COLS), 1.0 if index % 4 == 3 else 0.0, jnp.float32)

    def slice_step(z, carry):
        k = shift_ref[1, z] + 64
        here = d_ref[z]
        behind = jnp.concatenate([pltpu.roll(d_ref[z, 0:8, :], 1, 0), d_ref[z, 7:63, :]], axis=0)
        mixed = here + frac_ref[0, z] * (behind - here)
        left = pltpu.roll(mixed, 1, 1)
        sheared = pltpu.roll(mixed + frac_ref[1, z] * (left - mixed), k, 1)
        tints = tint(sheared)
        keep = jnp.exp((-absorb_ref[z] * scale) * softplus(sheared))
        keep = jnp.concatenate([jnp.where(sub == 0, 1.0, keep[0:8]), keep[8:]], axis=0)
        view = acc_ref.at[:, pl.ds(shift_ref[0, z] + 64, 64), :]
        absorb_sample(view, 0, tints, jnp.where(lane > k, keep, 1.0))
        absorb_sample(view, 1, tints, jnp.where(lane < k, keep, 1.0))
        return carry

    lax.fori_loop(0, SLAB, slice_step, 0, unroll=SLICE_UNROLL)

    odd = edge_ref[0]
    for start, out_ref in ((128 - 128 * odd, near_ref), (64, own_ref), (128 * odd, far_ref)):
        for half in range(2):
            for channel in range(4):
                value = acc_ref[4 * half + channel, pl.ds(pl.multiple_of(start, 64), 64), :]
                value = 1.0 - value if channel == 3 else value
                out_ref[pl.ds(64 * (4 * half + channel), 64), :] = value
    near_ref[pl.ds(512, 64), :] = rows_ref[pl.ds(pl.multiple_of(64 * odd, 64), 64), :]
    far_ref[pl.ds(512, 64), :] = rows_ref[pl.ds(pl.multiple_of(64 - 64 * odd, 64), 64), :]
    near_ref[pl.ds(576, 64), :] = cols_ref[...]
    far_ref[pl.ds(576, 64), :] = cols_ref[...]


def over(front, behind):
    through = 1.0 - front[3]
    return [front[c] + through * behind[c] for c in range(4)]


def channels(ref, *index):
    return [ref[(*index, c)] for c in range(4)]


def turn_rows(plane, amounts):
    sub = lax.broadcasted_iota(jnp.int32, (8, COLS), 0)
    tiles = []
    for t in range(plane.shape[0] // 8):
        tile = plane[8 * t : 8 * t + 8]
        turned = pltpu.roll(tile, amounts(8 * t), 1)
        for r in range(1, 8):
            turned = jnp.where(sub == r, pltpu.roll(tile, amounts(8 * t + r), 1), turned)
        tiles.append(turned)
    return jnp.concatenate(tiles, axis=0)


def exact_dot(a, b):
    return jnp.dot(a, b, precision=lax.Precision.HIGHEST, preferred_element_type=jnp.float32)


def line_composite(sheared, opticals, key_row, key_col):
    first = lax.broadcasted_iota(jnp.int32, (SLAB, SLAB), 0)
    second = lax.broadcasted_iota(jnp.int32, (SLAB, SLAB), 1)
    ahead = jnp.where((second < first) & (key_row == key_col), 1.0, 0.0)
    target = lax.broadcasted_iota(jnp.int32, (2 * SLAB, SLAB), 0).astype(jnp.float32)
    chosen = jnp.where(target == key_row + 64.0, 1.0, 0.0)
    before = exact_dot(ahead, jnp.concatenate(opticals, axis=1))
    tints = tint(sheared)
    pieces = []
    for half, optical in enumerate(opticals):
        front = before[:, COLS * half : COLS * half + COLS]
        weight = jnp.exp(-front) - jnp.exp(-(front + optical))
        pieces += [weight * tints[0], weight * tints[1], weight * tints[2], weight]
    total = exact_dot(chosen, jnp.concatenate(pieces, axis=1))
    return [total[:, COLS * p : COLS * p + COLS] for p in range(len(pieces))]


def rows_kernel(
    scale, shift_ref, edge_ref, own_ref, near_ref, far_ref, rows_ref, cols_ref, fvec_ref, fcol_ref,
    mine_ref, near_out_ref, far_out_ref, u_ref,
):
    lane = lax.broadcasted_iota(jnp.int32, (1, COLS), 1)
    odd_row, odd_col = edge_ref[0] == 1, edge_ref[1] == 1
    fy, fx, rate = fcol_ref[:, 0:1], fcol_ref[:, 1:2], fcol_ref[:, 2:3] * scale
    oy, ox = fcol_ref[:, 3:4], fcol_ref[:, 4:5]

    def received(start, size):
        near, far = near_ref[pl.ds(start, size), :], far_ref[pl.ds(start, size), :]
        return jnp.where(odd_row, far, near), jnp.where(odd_row, near, far)

    below_row, above_row = received(512, 64)
    here = jnp.where(oy < 0.0, below_row, rows_ref[pl.ds(64, 64), :])
    behind = jnp.where(oy < 0.0, rows_ref[pl.ds(0, 64), :], above_row)
    mixed = here + fy * (behind - here)
    sheared = mixed + fx * (pltpu.roll(mixed, 1, 1) - mixed)
    sheared = turn_rows(sheared, lambda z: shift_ref[1, z] + 64)
    optical = rate * softplus(sheared)
    place = lane.astype(jnp.float32)
    opticals = [jnp.where(place > ox + 64.0, optical, 0.0), jnp.where(place < ox + 64.0, optical, 0.0)]
    line = line_composite(sheared, opticals, fvec_ref[3:4, 0:SLAB], oy)

    halves = []
    for half in range(2):
        pairs = [received(64 * (4 * half + c), 64) for c in range(4)]
        own = [own_ref[pl.ds(64 * (4 * half + c), 64), :] for c in range(4)]
        lower = [line[4 * half + c][:64] for c in range(4)]
        upper = [line[4 * half + c][64:] for c in range(4)]
        merged = over(own, over(upper, [above for _, above in pairs]))
        halves.append(over([below for below, _ in pairs], over(lower, merged)))
    for c in range(4):
        low, high = halves[0][c], halves[1][c]
        low_turned, high_turned = pltpu.roll(low, 64, 1), pltpu.roll(high, 64, 1)
        mine_ref[c] = jnp.where(lane < 64, low_turned, high_turned)
        left = jnp.where(lane < 64, low[:32], low_turned[32:])
        right = jnp.where(lane < 64, high_turned[:32], high[32:])
        near_out_ref[pl.ds(32 * c, 32), :] = jnp.where(odd_col, left, right)
        far_out_ref[pl.ds(32 * c, 32), :] = jnp.where(odd_col, right, left)

    below_col, above_col = received(576, 64)
    negative = jnp.concatenate([fvec_ref[3:4, 0:SLAB]] * 2, axis=1) < 0.0
    pair = jnp.concatenate(
        [jnp.where(negative, cols_ref[...], above_col), jnp.where(negative, below_col, cols_ref[...])], axis=0
    )

    def amount(z):
        offset = shift_ref[0, z % SLAB]
        return jnp.where(offset < 0, offset + COLS, offset + 64)

    here = turn_rows(jnp.transpose(pair), amount)
    columns = here + jnp.concatenate([fy, fy], axis=0) * (pltpu.roll(here, 1, 1) - here)
    u_ref[...] = columns
    near_out_ref[pl.ds(128, 64), :] = jnp.where(odd_col, columns[64:], columns[:64])
    far_out_ref[pl.ds(128, 64), :] = jnp.where(odd_col, columns[:64], columns[64:])


def columns_kernel(scale, limit, edge_ref, mine_ref, near_ref, far_ref, u_ref, zrow_ref, zcol_ref, fvec_ref, fcol_ref, out_ref):
    lane = lax.broadcasted_iota(jnp.int32, (1, COLS), 1)
    odd_col = edge_ref[1] == 1
    fx, rate, oy, ox = fcol_ref[:, 1:2], fcol_ref[:, 2:3] * scale, fcol_ref[:, 3:4], fcol_ref[:, 4:5]

    def received(start, size):
        near, far = near_ref[pl.ds(start, size), :], far_ref[pl.ds(start, size), :]
        return jnp.where(odd_col, far, near), jnp.where(odd_col, near, far)

    right_first, left_last = received(128, 64)
    here = jnp.where(ox < 0.0, right_first, u_ref[pl.ds(64, 64), :])
    behind = jnp.where(ox < 0.0, u_ref[pl.ds(0, 64), :], left_last)
    sheared = here + fx * (behind - here)
    row = (lane + edge_ref[2]).astype(jnp.float32) - oy
    optical = jnp.where((row >= 0.0) & (row <= limit), rate * softplus(sheared), 0.0)
    line = line_composite(sheared, [optical], fvec_ref[4:5, 0:SLAB], ox)
    line = [pltpu.roll(jnp.transpose(part)[:64], 64, 1) for part in line]

    front, behind = [], []
    for c in range(4):
        right, left = received(32 * c, 32)
        upper = jnp.concatenate([pltpu.roll(right, 64, 1), right], axis=0)
        lower = jnp.concatenate([left, pltpu.roll(left, 64, 1)], axis=0)
        own = mine_ref[c]
        front.append(jnp.where(lane < 64, own, upper))
        behind.append(jnp.where(lane < 64, lower, own))
    inner = over(front, over(line, behind))
    total = jnp.sum(fvec_ref[2:3, :], axis=1, keepdims=True)
    pre = jnp.maximum(zrow_ref[:, 0:1], zcol_ref[0:1, :])
    post = jnp.minimum(jnp.maximum(zrow_ref[:, 1:2], zcol_ref[1:2, :]), total - pre)
    flat = []
    for amount in (pre, jnp.maximum(post, 0.0)):
        fade = 1.0 - jnp.exp((-scale * LN2) * amount)
        flat.append([jnp.zeros_like(fade), fade, math.tanh(0.4) * fade, fade])
    whole = over(flat[0], over(inner, flat[1]))
    pieces = out_ref.shape[0]
    height = ROWS // pieces
    for p in range(pieces):
        for c in range(4):
            out_ref[p, c] = whole[c][p * height : (p + 1) * height]


def fold_kernel(in_ref, out_ref):
    merged = channels(in_ref, 0)
    for slab in range(1, in_ref.shape[0]):
        merged = over(merged, channels(in_ref, slab))
    out_ref[0] = 0.5 * (merged[3] + merged[0])
    out_ref[1] = merged[1]
    out_ref[2] = 0.5 * (merged[3] + merged[2])
    out_ref[3] = merged[3]


def matching(count, first):
    pairs = [(i, i + 1) for i in range(first, count - 1, 2)]
    return pairs + [(j, i) for i, j in pairs]


def body(coefficients, shifts, fraction, absorb):
    depth_count = lax.axis_size("depth")
    row_count = lax.axis_size("imgy")
    col_count = lax.axis_size("imgx")
    scale = 2.0 / (SLAB * depth_count)
    iy, ix = lax.axis_index("imgy"), lax.axis_index("imgx")

    shift_rows, shift_cols = shifts[0], shifts[1]
    edge = jnp.stack([iy % 2, ix % 2, iy * ROWS]).astype(jnp.int32)
    lines = jnp.concatenate([fraction, absorb[None], shifts.astype(jnp.float32)], axis=0)
    vectors = jnp.pad(lines, ((0, 3), (0, COLS - SLAB)))
    columns = jnp.pad(lines.T, ((0, 0), (0, 3)))

    sent = f32(640, COLS)
    near, own, far, row_planes, col_planes = call(
        functools.partial(tile_kernel, scale),
        (sent, f32(512, COLS), sent, f32(128, COLS), f32(64, COLS)),
        [SMEM_SPEC] * 4 + [VMEM_SPEC],
        [
            pltpu.VMEM((16, 16, COLS), jnp.float32),
            pltpu.VMEM((32, 32, COLS), jnp.float32),
            pltpu.VMEM((64, 64, COLS), jnp.float32),
            pltpu.VMEM((64, COLS), jnp.float32),
            pltpu.VMEM((8, EXT, COLS), jnp.float32),
        ],
        flops=300_000_000,
        bytes_moved=4 << 20,
    )(shifts, fraction, absorb, edge, coefficients)

    near = lax.ppermute(near, "imgy", matching(row_count, 0))
    far = lax.ppermute(far, "imgy", matching(row_count, 1))
    packed = f32(192, COLS)
    mine, near, far, sheared_cols = call(
        functools.partial(rows_kernel, scale),
        (f32(4, ROWS, COLS), packed, packed, f32(128, COLS)),
        [SMEM_SPEC] * 2 + [VMEM_SPEC] * 7,
    )(shifts, edge, own, near, far, row_planes, col_planes, vectors, columns)
    near = lax.ppermute(near, "imgx", matching(col_count, 0))
    far = lax.ppermute(far, "imgx", matching(col_count, 1))

    image_rows = iy * ROWS + jnp.arange(ROWS, dtype=jnp.int32)
    image_cols = ix * COLS + jnp.arange(COLS, dtype=jnp.int32)

    def outside(pixels, offsets, limit):
        position = pixels[:, None] - offsets[None, :]
        pre = jnp.sum(jnp.where(position > limit, absorb[None, :], 0.0), axis=1)
        post = jnp.sum(jnp.where(position < 0, absorb[None, :], 0.0), axis=1)
        return pre, post

    zrow = jnp.stack(outside(image_rows, shift_rows, ROWS * row_count), axis=1)
    zcol = jnp.stack(outside(image_cols, shift_cols, COLS * col_count), axis=0)
    pieces = call(
        functools.partial(columns_kernel, scale, float(ROWS * row_count)),
        f32(depth_count, 4, ROWS // depth_count, COLS),
        [SMEM_SPEC] + [VMEM_SPEC] * 8,
    )(edge, mine, near, far, sheared_cols, zrow, zcol, vectors, columns)
    incoming = lax.all_to_all(pieces, "depth", split_axis=0, concat_axis=0, tiled=True)
    image = call(fold_kernel, f32(4, ROWS // depth_count, COLS), [VMEM_SPEC])(incoming)
    return image[:, None]


def solution(mesh):
    in_specs = (P("depth", "imgy", "imgx"), P(None, "depth"), P(None, "depth"), P("depth"))
    out_specs = P(None, "imgy", "depth", "imgx")
    return jax.shard_map(body, mesh=mesh, in_specs=in_specs, out_specs=out_specs, check_vma=False)
```

```python
import functools
import math

import jax
import jax.numpy as jnp
from jax import lax
from jax.experimental import pallas as pl
from jax.experimental.pallas import tpu as pltpu
from jax.sharding import PartitionSpec as P

BRICK = 64
SLAB = 64
ROWS = 64
COLS = 128
EXT = 208
SLICE_UNROLL = 8
LN2 = math.log(2.0)
VMEM_SPEC = pl.BlockSpec(memory_space=pltpu.VMEM)
SMEM_SPEC = pl.BlockSpec(memory_space=pltpu.SMEM)
HBM_SPEC = pl.BlockSpec(memory_space=pltpu.HBM)
CHUNK = 16
INTERPRET = False


def call(kernel, out_shape, in_specs, scratch=(), flops=1000, bytes_moved=1000):
    specs = jax.tree.map(lambda _: VMEM_SPEC, out_shape)
    return pl.pallas_call(
        kernel,
        out_shape=out_shape,
        in_specs=in_specs,
        out_specs=specs,
        scratch_shapes=list(scratch),
        interpret=INTERPRET,
        compiler_params=pltpu.CompilerParams(vmem_limit_bytes=24 << 20),
        cost_estimate=pl.CostEstimate(flops=flops, bytes_accessed=bytes_moved, transcendentals=0),
    )


def f32(*shape):
    return jax.ShapeDtypeStruct(shape, jnp.float32)


def lane_table(half):
    source = lax.broadcasted_iota(jnp.int32, (2 * COLS, COLS), 0) % COLS
    target = lax.broadcasted_iota(jnp.int32, (2 * COLS, COLS), 1)
    local = target % BRICK
    start = target - local
    pair = local // 2
    weight = jnp.where(local % 2 == 1, 0.5, -0.5)
    inside = local < 2 * half
    low = jnp.where(inside & (source == start + pair), 1.0, 0.0)
    high = jnp.where(inside & (source == start + half + pair), weight, 0.0)
    return (low + high).astype(jnp.bfloat16)


def lane_lift(block, table):
    coarse = block.astype(jnp.bfloat16)
    rest = (block - coarse.astype(jnp.float32)).astype(jnp.bfloat16)
    both = jnp.concatenate([coarse, rest], axis=1)
    return jnp.dot(both, table, preferred_element_type=jnp.float32)


def softplus(sheared):
    return jnp.maximum(sheared, 0.0) + jnp.log(1.0 + jnp.exp(-jnp.abs(sheared)))


def tint(sheared):
    return jnp.tanh(0.75 * sheared), jnp.exp(-0.5 * (sheared * sheared)), jnp.tanh(0.4 - 0.5 * sheared)


def absorb_sample(view, half, tints, keep):
    through = view[4 * half + 3]
    after = through * keep
    weight = through - after
    view[4 * half + 3] = after
    for channel in range(3):
        view[4 * half + channel] = view[4 * half + channel] + weight * tints[channel]


def tile_kernel(
    scale, edge_ref, shift_hbm, frac_hbm, absorb_hbm, c_hbm, near_ref, own_ref, far_ref, rows_ref, cols_ref,
    shift_ref, frac_ref, absorb_ref, c_ref, s2_ref, s1_ref, d_ref, plane_ref, acc_ref, sems,
):
    loads = [
        pltpu.make_async_copy(c_hbm.at[pl.ds(CHUNK * i, CHUNK)], c_ref.at[pl.ds(CHUNK * i, CHUNK)], sems.at[i])
        for i in range(SLAB // CHUNK)
    ]
    scalars = [
        pltpu.make_async_copy(shift_hbm, shift_ref, sems.at[4]),
        pltpu.make_async_copy(frac_hbm, frac_ref, sems.at[5]),
        pltpu.make_async_copy(absorb_hbm, absorb_ref, sems.at[6]),
    ]
    for copy in loads + scalars:
        copy.start()
    for index in range(8):
        acc_ref[index] = jnp.full((EXT, COLS), 1.0 if index % 4 == 3 else 0.0, jnp.float32)

    lane = lax.broadcasted_iota(jnp.int32, (1, COLS), 1)
    sub = lax.broadcasted_iota(jnp.int32, (8, COLS), 0)

    def level(half, below, out_ref, on_result, init, unroll, span=None):
        table = lane_table(half)

        def step(i, carry):
            if below is None:
                low = c_ref[i, : 2 * half, :]
            else:
                corner = jnp.where(lane % BRICK < half, below[i], c_ref[i, :half, :])
                low = jnp.concatenate([corner, c_ref[i, half : 2 * half, :]], axis=0)
            high = c_ref[i + half, : 2 * half, :]
            planes = []
            even = low - 0.5 * high
            for part in (even, even + high):
                row_even = part[:half] - 0.5 * part[half:]
                planes += [row_even, row_even + part[half:]]
            result = lane_lift(jnp.concatenate(planes, axis=0), table)
            for odd in range(2):
                for row_odd in range(2):
                    start = (2 * odd + row_odd) * half
                    out_ref[2 * i + odd, pl.ds(row_odd, half, stride=2), :] = result[start : start + half]
            return on_result(i, result, carry)

        first, last = span or (0, half)
        return lax.fori_loop(first, last, step, init, unroll=unroll)

    def ignore(i, result, carry):
        return carry

    def boundary(i, result, plane):
        for odd in range(2):
            z = 2 * i + odd
            piece = result[64 * odd : 64 * odd + 64]
            rows_ref[pl.ds(z, 1), :] = piece[63:64]
            rows_ref[pl.ds(64 + z, 1), :] = piece[0:1]
            plane = jnp.where(lane == z, pltpu.roll(piece, z + 1, 1), plane)
            plane = jnp.where(lane == z + 64, pltpu.roll(piece, z + 64, 1), plane)
        return plane

    loads[0].wait()
    level(8, None, s2_ref, ignore, 0, 8)
    loads[1].wait()
    level(16, s2_ref, s1_ref, ignore, 0, 16)
    loads[2].wait()
    plane = level(32, s1_ref, d_ref, boundary, jnp.zeros((64, COLS), jnp.float32), 16, (0, 16))
    loads[3].wait()
    plane_ref[...] = level(32, s1_ref, d_ref, boundary, plane, 16, (16, 32))
    for row_odd in range(2):
        cols_ref[pl.ds(row_odd, 32, stride=2), :] = plane_ref[pl.ds(32 * row_odd, 32), :]

    for copy in scalars:
        copy.wait()

    def slice_step(z, carry):
        k = shift_ref[1, z] + 64
        here = d_ref[z]
        behind = jnp.concatenate([pltpu.roll(d_ref[z, 0:8, :], 1, 0), d_ref[z, 7:63, :]], axis=0)
        mixed = here + frac_ref[0, z] * (behind - here)
        left = pltpu.roll(mixed, 1, 1)
        sheared = pltpu.roll(mixed + frac_ref[1, z] * (left - mixed), k, 1)
        tints = tint(sheared)
        keep = jnp.exp((-absorb_ref[z] * scale) * softplus(sheared))
        keep = jnp.concatenate([jnp.where(sub == 0, 1.0, keep[0:8]), keep[8:]], axis=0)
        view = acc_ref.at[:, pl.ds(shift_ref[0, z] + 64, 64), :]
        absorb_sample(view, 0, tints, jnp.where(lane > k, keep, 1.0))
        absorb_sample(view, 1, tints, jnp.where(lane < k, keep, 1.0))
        return carry

    lax.fori_loop(0, SLAB, slice_step, 0, unroll=SLICE_UNROLL)

    odd = edge_ref[0]
    for start, out_ref in ((128 - 128 * odd, near_ref), (64, own_ref), (128 * odd, far_ref)):
        for half in range(2):
            for channel in range(4):
                value = acc_ref[4 * half + channel, pl.ds(pl.multiple_of(start, 64), 64), :]
                value = 1.0 - value if channel == 3 else value
                out_ref[pl.ds(64 * (4 * half + channel), 64), :] = value
    near_ref[pl.ds(512, 64), :] = rows_ref[pl.ds(pl.multiple_of(64 * odd, 64), 64), :]
    far_ref[pl.ds(512, 64), :] = rows_ref[pl.ds(pl.multiple_of(64 - 64 * odd, 64), 64), :]
    near_ref[pl.ds(576, 64), :] = cols_ref[...]
    far_ref[pl.ds(576, 64), :] = cols_ref[...]


def over(front, behind):
    through = 1.0 - front[3]
    return [front[c] + through * behind[c] for c in range(4)]


def channels(ref, *index):
    return [ref[(*index, c)] for c in range(4)]


def turn_rows(plane, amounts):
    sub = lax.broadcasted_iota(jnp.int32, (8, COLS), 0)
    tiles = []
    for t in range(plane.shape[0] // 8):
        tile = plane[8 * t : 8 * t + 8]
        turned = pltpu.roll(tile, amounts(8 * t), 1)
        for r in range(1, 8):
            turned = jnp.where(sub == r, pltpu.roll(tile, amounts(8 * t + r), 1), turned)
        tiles.append(turned)
    return jnp.concatenate(tiles, axis=0)


def exact_dot(a, b):
    return jnp.dot(a, b, precision=lax.Precision.HIGHEST, preferred_element_type=jnp.float32)


def line_composite(sheared, opticals, key_row, key_col):
    first = lax.broadcasted_iota(jnp.int32, (SLAB, SLAB), 0)
    second = lax.broadcasted_iota(jnp.int32, (SLAB, SLAB), 1)
    ahead = jnp.where((second < first) & (key_row == key_col), 1.0, 0.0)
    target = lax.broadcasted_iota(jnp.int32, (2 * SLAB, SLAB), 0).astype(jnp.float32)
    chosen = jnp.where(target == key_row + 64.0, 1.0, 0.0)
    before = exact_dot(ahead, jnp.concatenate(opticals, axis=1))
    tints = tint(sheared)
    pieces = []
    for half, optical in enumerate(opticals):
        front = before[:, COLS * half : COLS * half + COLS]
        weight = jnp.exp(-front) - jnp.exp(-(front + optical))
        pieces += [weight * tints[0], weight * tints[1], weight * tints[2], weight]
    total = exact_dot(chosen, jnp.concatenate(pieces, axis=1))
    return [total[:, COLS * p : COLS * p + COLS] for p in range(len(pieces))]


def rows_kernel(
    scale, shift_ref, edge_ref, own_ref, near_ref, far_ref, rows_ref, cols_ref, fvec_ref, fcol_ref,
    mine_ref, near_out_ref, far_out_ref, u_ref,
):
    lane = lax.broadcasted_iota(jnp.int32, (1, COLS), 1)
    odd_row, odd_col = edge_ref[0] == 1, edge_ref[1] == 1
    fy, fx, rate = fcol_ref[:, 0:1], fcol_ref[:, 1:2], fcol_ref[:, 2:3] * scale
    oy, ox = fcol_ref[:, 3:4], fcol_ref[:, 4:5]

    def received(start, size):
        near, far = near_ref[pl.ds(start, size), :], far_ref[pl.ds(start, size), :]
        return jnp.where(odd_row, far, near), jnp.where(odd_row, near, far)

    below_row, above_row = received(512, 64)
    here = jnp.where(oy < 0.0, below_row, rows_ref[pl.ds(64, 64), :])
    behind = jnp.where(oy < 0.0, rows_ref[pl.ds(0, 64), :], above_row)
    mixed = here + fy * (behind - here)
    sheared = mixed + fx * (pltpu.roll(mixed, 1, 1) - mixed)
    sheared = turn_rows(sheared, lambda z: shift_ref[1, z] + 64)
    optical = rate * softplus(sheared)
    place = lane.astype(jnp.float32)
    opticals = [jnp.where(place > ox + 64.0, optical, 0.0), jnp.where(place < ox + 64.0, optical, 0.0)]
    line = line_composite(sheared, opticals, fvec_ref[3:4, 0:SLAB], oy)

    halves = []
    for half in range(2):
        pairs = [received(64 * (4 * half + c), 64) for c in range(4)]
        own = [own_ref[pl.ds(64 * (4 * half + c), 64), :] for c in range(4)]
        lower = [line[4 * half + c][:64] for c in range(4)]
        upper = [line[4 * half + c][64:] for c in range(4)]
        merged = over(own, over(upper, [above for _, above in pairs]))
        halves.append(over([below for below, _ in pairs], over(lower, merged)))
    for c in range(4):
        low, high = halves[0][c], halves[1][c]
        low_turned, high_turned = pltpu.roll(low, 64, 1), pltpu.roll(high, 64, 1)
        mine_ref[c] = jnp.where(lane < 64, low_turned, high_turned)
        left = jnp.where(lane < 64, low[:32], low_turned[32:])
        right = jnp.where(lane < 64, high_turned[:32], high[32:])
        near_out_ref[pl.ds(32 * c, 32), :] = jnp.where(odd_col, left, right)
        far_out_ref[pl.ds(32 * c, 32), :] = jnp.where(odd_col, right, left)

    below_col, above_col = received(576, 64)
    negative = jnp.concatenate([fvec_ref[3:4, 0:SLAB]] * 2, axis=1) < 0.0
    pair = jnp.concatenate(
        [jnp.where(negative, cols_ref[...], above_col), jnp.where(negative, below_col, cols_ref[...])], axis=0
    )

    def amount(z):
        offset = shift_ref[0, z % SLAB]
        return jnp.where(offset < 0, offset + COLS, offset + 64)

    here = turn_rows(jnp.transpose(pair), amount)
    columns = here + jnp.concatenate([fy, fy], axis=0) * (pltpu.roll(here, 1, 1) - here)
    u_ref[...] = columns
    near_out_ref[pl.ds(128, 64), :] = jnp.where(odd_col, columns[64:], columns[:64])
    far_out_ref[pl.ds(128, 64), :] = jnp.where(odd_col, columns[:64], columns[64:])


def columns_kernel(scale, limit, edge_ref, mine_ref, near_ref, far_ref, u_ref, zrow_ref, zcol_ref, fvec_ref, fcol_ref, out_ref):
    lane = lax.broadcasted_iota(jnp.int32, (1, COLS), 1)
    odd_col = edge_ref[1] == 1
    fx, rate, oy, ox = fcol_ref[:, 1:2], fcol_ref[:, 2:3] * scale, fcol_ref[:, 3:4], fcol_ref[:, 4:5]

    def received(start, size):
        near, far = near_ref[pl.ds(start, size), :], far_ref[pl.ds(start, size), :]
        return jnp.where(odd_col, far, near), jnp.where(odd_col, near, far)

    right_first, left_last = received(128, 64)
    here = jnp.where(ox < 0.0, right_first, u_ref[pl.ds(64, 64), :])
    behind = jnp.where(ox < 0.0, u_ref[pl.ds(0, 64), :], left_last)
    sheared = here + fx * (behind - here)
    row = (lane + edge_ref[2]).astype(jnp.float32) - oy
    optical = jnp.where((row >= 0.0) & (row <= limit), rate * softplus(sheared), 0.0)
    line = line_composite(sheared, [optical], fvec_ref[4:5, 0:SLAB], ox)
    line = [pltpu.roll(jnp.transpose(part)[:64], 64, 1) for part in line]

    front, behind = [], []
    for c in range(4):
        right, left = received(32 * c, 32)
        upper = jnp.concatenate([pltpu.roll(right, 64, 1), right], axis=0)
        lower = jnp.concatenate([left, pltpu.roll(left, 64, 1)], axis=0)
        own = mine_ref[c]
        front.append(jnp.where(lane < 64, own, upper))
        behind.append(jnp.where(lane < 64, lower, own))
    inner = over(front, over(line, behind))
    total = jnp.sum(fvec_ref[2:3, :], axis=1, keepdims=True)
    pre = jnp.maximum(zrow_ref[:, 0:1], zcol_ref[0:1, :])
    post = jnp.minimum(jnp.maximum(zrow_ref[:, 1:2], zcol_ref[1:2, :]), total - pre)
    flat = []
    for amount in (pre, jnp.maximum(post, 0.0)):
        fade = 1.0 - jnp.exp((-scale * LN2) * amount)
        flat.append([jnp.zeros_like(fade), fade, math.tanh(0.4) * fade, fade])
    whole = over(flat[0], over(inner, flat[1]))
    pieces = out_ref.shape[0]
    height = ROWS // pieces
    for p in range(pieces):
        for c in range(4):
            out_ref[p, c] = whole[c][p * height : (p + 1) * height]


def fold_kernel(in_ref, out_ref):
    merged = channels(in_ref, 0)
    for slab in range(1, in_ref.shape[0]):
        merged = over(merged, channels(in_ref, slab))
    out_ref[0] = 0.5 * (merged[3] + merged[0])
    out_ref[1] = merged[1]
    out_ref[2] = 0.5 * (merged[3] + merged[2])
    out_ref[3] = merged[3]


def matching(count, first):
    pairs = [(i, i + 1) for i in range(first, count - 1, 2)]
    return pairs + [(j, i) for i, j in pairs]


def body(coefficients, shifts, fraction, absorb):
    depth_count = lax.axis_size("depth")
    row_count = lax.axis_size("imgy")
    col_count = lax.axis_size("imgx")
    scale = 2.0 / (SLAB * depth_count)
    iy, ix = lax.axis_index("imgy"), lax.axis_index("imgx")

    shift_rows, shift_cols = shifts[0], shifts[1]
    edge = jnp.stack([iy % 2, ix % 2, iy * ROWS]).astype(jnp.int32)
    lines = jnp.concatenate([fraction, absorb[None], shifts.astype(jnp.float32)], axis=0)
    vectors = jnp.pad(lines, ((0, 3), (0, COLS - SLAB)))
    columns = jnp.pad(lines.T, ((0, 0), (0, 3)))

    sent = f32(640, COLS)
    near, own, far, row_planes, col_planes = call(
        functools.partial(tile_kernel, scale),
        (sent, f32(512, COLS), sent, f32(128, COLS), f32(64, COLS)),
        [SMEM_SPEC] + [HBM_SPEC] * 4,
        [
            pltpu.SMEM((2, SLAB), jnp.int32),
            pltpu.SMEM((2, SLAB), jnp.float32),
            pltpu.SMEM((SLAB,), jnp.float32),
            pltpu.VMEM((SLAB, ROWS, COLS), jnp.float32),
            pltpu.VMEM((16, 16, COLS), jnp.float32),
            pltpu.VMEM((32, 32, COLS), jnp.float32),
            pltpu.VMEM((64, 64, COLS), jnp.float32),
            pltpu.VMEM((64, COLS), jnp.float32),
            pltpu.VMEM((8, EXT, COLS), jnp.float32),
            pltpu.SemaphoreType.DMA((7,)),
        ],
        flops=300_000_000,
        bytes_moved=4 << 20,
    )(edge, *[pltpu.with_memory_space_constraint(a, pltpu.HBM) for a in (shifts, fraction, absorb, coefficients)])

    far = lax.ppermute(far, "imgy", matching(row_count, 1))
    near = lax.ppermute(near, "imgy", matching(row_count, 0))
    packed = f32(192, COLS)
    mine, near, far, sheared_cols = call(
        functools.partial(rows_kernel, scale),
        (f32(4, ROWS, COLS), packed, packed, f32(128, COLS)),
        [SMEM_SPEC] * 2 + [VMEM_SPEC] * 7,
    )(shifts, edge, own, near, far, row_planes, col_planes, vectors, columns)
    far = lax.ppermute(far, "imgx", matching(col_count, 1))
    near = lax.ppermute(near, "imgx", matching(col_count, 0))

    image_rows = iy * ROWS + jnp.arange(ROWS, dtype=jnp.int32)
    image_cols = ix * COLS + jnp.arange(COLS, dtype=jnp.int32)

    def outside(pixels, offsets, limit):
        position = pixels[:, None] - offsets[None, :]
        pre = jnp.sum(jnp.where(position > limit, absorb[None, :], 0.0), axis=1)
        post = jnp.sum(jnp.where(position < 0, absorb[None, :], 0.0), axis=1)
        return pre, post

    zrow = jnp.stack(outside(image_rows, shift_rows, ROWS * row_count), axis=1)
    zcol = jnp.stack(outside(image_cols, shift_cols, COLS * col_count), axis=0)
    pieces = call(
        functools.partial(columns_kernel, scale, float(ROWS * row_count)),
        f32(depth_count, 4, ROWS // depth_count, COLS),
        [SMEM_SPEC] + [VMEM_SPEC] * 8,
    )(edge, mine, near, far, sheared_cols, zrow, zcol, vectors, columns)
    incoming = lax.all_to_all(pieces, "depth", split_axis=0, concat_axis=0, tiled=True)
    image = call(fold_kernel, f32(4, ROWS // depth_count, COLS), [VMEM_SPEC])(incoming)
    return image[:, None]


def solution(mesh):
    in_specs = (P("depth", "imgy", "imgx"), P(None, "depth"), P(None, "depth"), P("depth"))
    out_specs = P(None, "imgy", "depth", "imgx")
    return jax.shard_map(body, mesh=mesh, in_specs=in_specs, out_specs=out_specs, check_vma=False)
```

```python
import functools
import math

import jax
import jax.numpy as jnp
from jax import lax
from jax.experimental import pallas as pl
from jax.experimental.pallas import tpu as pltpu
from jax.sharding import PartitionSpec as P

BRICK = 64
SLAB = 64
ROWS = 64
COLS = 128
EXT = 208
SLICE_UNROLL = 8
LN2 = math.log(2.0)
LOG2E = 1.0 / math.log(2.0)
VMEM_SPEC = pl.BlockSpec(memory_space=pltpu.VMEM)
SMEM_SPEC = pl.BlockSpec(memory_space=pltpu.SMEM)
HBM_SPEC = pl.BlockSpec(memory_space=pltpu.HBM)
CHUNK = 16
INTERPRET = False


def call(kernel, out_shape, in_specs, scratch=(), flops=1000, bytes_moved=1000):
    specs = jax.tree.map(lambda _: VMEM_SPEC, out_shape)
    return pl.pallas_call(
        kernel,
        out_shape=out_shape,
        in_specs=in_specs,
        out_specs=specs,
        scratch_shapes=list(scratch),
        interpret=INTERPRET,
        compiler_params=pltpu.CompilerParams(vmem_limit_bytes=24 << 20),
        cost_estimate=pl.CostEstimate(flops=flops, bytes_accessed=bytes_moved, transcendentals=0),
    )


def f32(*shape):
    return jax.ShapeDtypeStruct(shape, jnp.float32)


def lane_table(half):
    source = lax.broadcasted_iota(jnp.int32, (2 * COLS, COLS), 0) % COLS
    target = lax.broadcasted_iota(jnp.int32, (2 * COLS, COLS), 1)
    local = target % BRICK
    start = target - local
    pair = local // 2
    weight = jnp.where(local % 2 == 1, 0.5, -0.5)
    inside = local < 2 * half
    low = jnp.where(inside & (source == start + pair), 1.0, 0.0)
    high = jnp.where(inside & (source == start + half + pair), weight, 0.0)
    return (low + high).astype(jnp.bfloat16)


def lane_lift(block, table):
    coarse = block.astype(jnp.bfloat16)
    rest = (block - coarse.astype(jnp.float32)).astype(jnp.bfloat16)
    both = jnp.concatenate([coarse, rest], axis=1)
    return jnp.dot(both, table, preferred_element_type=jnp.float32)


def softplus(sheared):
    return jnp.maximum(sheared, 0.0) + jnp.log(1.0 + jnp.exp(-jnp.abs(sheared)))


def tint(sheared):
    return jnp.tanh(0.75 * sheared), jnp.exp(-0.5 * (sheared * sheared)), jnp.tanh(0.4 - 0.5 * sheared)


def tile_kernel(
    scale, edge_ref, shift_hbm, frac_hbm, absorb_hbm, c_hbm, near_ref, own_ref, far_ref, rows_ref, cols_ref,
    shift_ref, frac_ref, absorb_ref, c_ref, s2_ref, s1_ref, d_ref, plane_ref, acc_ref, sems,
):
    loads = [
        pltpu.make_async_copy(c_hbm.at[pl.ds(CHUNK * i, CHUNK)], c_ref.at[pl.ds(CHUNK * i, CHUNK)], sems.at[i])
        for i in range(SLAB // CHUNK)
    ]
    scalars = [
        pltpu.make_async_copy(shift_hbm, shift_ref, sems.at[4]),
        pltpu.make_async_copy(frac_hbm, frac_ref, sems.at[5]),
        pltpu.make_async_copy(absorb_hbm, absorb_ref, sems.at[6]),
    ]
    for copy in loads + scalars:
        copy.start()
    for index in range(8):
        acc_ref[index] = jnp.full((EXT, COLS), 1.0 if index % 4 == 3 else 0.0, jnp.float32)

    lane = lax.broadcasted_iota(jnp.int32, (1, COLS), 1)
    sub = lax.broadcasted_iota(jnp.int32, (8, COLS), 0)

    def level(half, below, out_ref, on_result, init, unroll, span=None):
        table = lane_table(half)

        def step(i, carry):
            if below is None:
                low = c_ref[i, : 2 * half, :]
            else:
                corner = jnp.where(lane % BRICK < half, below[i], c_ref[i, :half, :])
                low = jnp.concatenate([corner, c_ref[i, half : 2 * half, :]], axis=0)
            high = c_ref[i + half, : 2 * half, :]
            planes = []
            even = low - 0.5 * high
            for part in (even, even + high):
                row_even = part[:half] - 0.5 * part[half:]
                planes += [row_even, row_even + part[half:]]
            result = lane_lift(jnp.concatenate(planes, axis=0), table)
            for odd in range(2):
                for row_odd in range(2):
                    start = (2 * odd + row_odd) * half
                    out_ref[2 * i + odd, pl.ds(row_odd, half, stride=2), :] = result[start : start + half]
            return on_result(i, result, carry)

        first, last = span or (0, half)
        return lax.fori_loop(first, last, step, init, unroll=unroll)

    def ignore(i, result, carry):
        return carry

    def boundary(i, result, plane):
        for odd in range(2):
            z = 2 * i + odd
            piece = result[64 * odd : 64 * odd + 64]
            rows_ref[pl.ds(z, 1), :] = piece[63:64]
            rows_ref[pl.ds(64 + z, 1), :] = piece[0:1]
            plane = jnp.where(lane == z, pltpu.roll(piece, z + 1, 1), plane)
            plane = jnp.where(lane == z + 64, pltpu.roll(piece, z + 64, 1), plane)
        return plane

    loads[0].wait()
    level(8, None, s2_ref, ignore, 0, 8)
    loads[1].wait()
    level(16, s2_ref, s1_ref, ignore, 0, 16)
    loads[2].wait()
    plane = level(32, s1_ref, d_ref, boundary, jnp.zeros((64, COLS), jnp.float32), 16, (0, 16))
    loads[3].wait()
    plane_ref[...] = level(32, s1_ref, d_ref, boundary, plane, 16, (16, 32))
    for row_odd in range(2):
        cols_ref[pl.ds(row_odd, 32, stride=2), :] = plane_ref[pl.ds(32 * row_odd, 32), :]

    for copy in scalars:
        copy.wait()

    inside = lax.broadcasted_iota(jnp.int32, (ROWS, COLS), 0) > 0

    def slice_step(z, carry):
        k = shift_ref[1, z] + 64
        here = d_ref[z]
        behind = jnp.concatenate([pltpu.roll(d_ref[z, 0:8, :], 1, 0), d_ref[z, 7:63, :]], axis=0)
        mixed = here + frac_ref[0, z] * (behind - here)
        left = pltpu.roll(mixed, 1, 1)
        sheared = pltpu.roll(mixed + frac_ref[1, z] * (left - mixed), k, 1)
        twos = LOG2E * sheared
        positive = jnp.maximum(twos, 0.0)
        soft = positive + jnp.log2(1.0 + jnp.exp2((twos - positive) - positive))
        keep = jnp.exp2((-absorb_ref[z] * scale) * soft)
        tints = jnp.tanh(0.75 * sheared), jnp.exp2((-0.5 * twos) * sheared), jnp.tanh(0.4 - 0.5 * sheared)
        view = acc_ref.at[:, pl.ds(shift_ref[0, z] + 64, 64), :]
        right = lane < k
        value = [jnp.where(right, view[4 + c], view[c]) for c in range(4)]
        after = value[3] * keep
        weight = value[3] - after
        value = [value[c] + weight * tints[c] for c in range(3)] + [after]
        for c in range(4):
            pltpu.store(view.at[c], value[c], mask=inside & (lane > k))
            pltpu.store(view.at[4 + c], value[c], mask=inside & right)
        return carry

    lax.fori_loop(0, SLAB, slice_step, 0, unroll=SLICE_UNROLL)

    odd = edge_ref[0]
    for start, out_ref in ((128 - 128 * odd, near_ref), (64, own_ref), (128 * odd, far_ref)):
        for half in range(2):
            for channel in range(4):
                value = acc_ref[4 * half + channel, pl.ds(pl.multiple_of(start, 64), 64), :]
                value = 1.0 - value if channel == 3 else value
                out_ref[pl.ds(64 * (4 * half + channel), 64), :] = value
    near_ref[pl.ds(512, 64), :] = rows_ref[pl.ds(pl.multiple_of(64 * odd, 64), 64), :]
    far_ref[pl.ds(512, 64), :] = rows_ref[pl.ds(pl.multiple_of(64 - 64 * odd, 64), 64), :]
    near_ref[pl.ds(576, 64), :] = cols_ref[...]
    far_ref[pl.ds(576, 64), :] = cols_ref[...]


def over(front, behind):
    through = 1.0 - front[3]
    return [front[c] + through * behind[c] for c in range(4)]


def channels(ref, *index):
    return [ref[(*index, c)] for c in range(4)]


def turn_rows(plane, amounts):
    sub = lax.broadcasted_iota(jnp.int32, (8, COLS), 0)
    tiles = []
    for t in range(plane.shape[0] // 8):
        tile = plane[8 * t : 8 * t + 8]
        turned = pltpu.roll(tile, amounts(8 * t), 1)
        for r in range(1, 8):
            turned = jnp.where(sub == r, pltpu.roll(tile, amounts(8 * t + r), 1), turned)
        tiles.append(turned)
    return jnp.concatenate(tiles, axis=0)


def select_dot(chosen, values):
    coarse = values.astype(jnp.bfloat16)
    rest = values - coarse.astype(jnp.float32)
    fine = rest.astype(jnp.bfloat16)
    left = chosen.astype(jnp.bfloat16)
    return jnp.dot(left, coarse, preferred_element_type=jnp.float32) + jnp.dot(
        left, fine, preferred_element_type=jnp.float32
    )


def line_composite(sheared, opticals, key_row, key_col):
    first = lax.broadcasted_iota(jnp.int32, (SLAB, SLAB), 0)
    second = lax.broadcasted_iota(jnp.int32, (SLAB, SLAB), 1)
    ahead = jnp.where((second < first) & (key_row == key_col), 1.0, 0.0)
    target = lax.broadcasted_iota(jnp.int32, (2 * SLAB, SLAB), 0).astype(jnp.float32)
    chosen = jnp.where(target == key_row + 64.0, 1.0, 0.0)
    before = select_dot(ahead, jnp.concatenate(opticals, axis=1))
    tints = tint(sheared)
    pieces = []
    for half, optical in enumerate(opticals):
        front = before[:, COLS * half : COLS * half + COLS]
        weight = jnp.exp(-front) - jnp.exp(-(front + optical))
        pieces += [weight * tints[0], weight * tints[1], weight * tints[2], weight]
    total = select_dot(chosen, jnp.concatenate(pieces, axis=1))
    return [total[:, COLS * p : COLS * p + COLS] for p in range(len(pieces))]


def rows_kernel(
    scale, shift_ref, edge_ref, own_ref, near_ref, far_ref, rows_ref, cols_ref, fvec_ref, fcol_ref,
    mine_ref, near_out_ref, far_out_ref, u_ref,
):
    lane = lax.broadcasted_iota(jnp.int32, (1, COLS), 1)
    odd_row, odd_col = edge_ref[0] == 1, edge_ref[1] == 1
    fy, fx, rate = fcol_ref[:, 0:1], fcol_ref[:, 1:2], fcol_ref[:, 2:3] * scale
    oy, ox = fcol_ref[:, 3:4], fcol_ref[:, 4:5]

    def received(start, size):
        near, far = near_ref[pl.ds(start, size), :], far_ref[pl.ds(start, size), :]
        return jnp.where(odd_row, far, near), jnp.where(odd_row, near, far)

    below_row, above_row = received(512, 64)
    here = jnp.where(oy < 0.0, below_row, rows_ref[pl.ds(64, 64), :])
    behind = jnp.where(oy < 0.0, rows_ref[pl.ds(0, 64), :], above_row)
    mixed = here + fy * (behind - here)
    sheared = mixed + fx * (pltpu.roll(mixed, 1, 1) - mixed)
    sheared = turn_rows(sheared, lambda z: shift_ref[1, z] + 64)
    optical = rate * softplus(sheared)
    place = lane.astype(jnp.float32)
    opticals = [jnp.where(place > ox + 64.0, optical, 0.0), jnp.where(place < ox + 64.0, optical, 0.0)]
    line = line_composite(sheared, opticals, fvec_ref[3:4, 0:SLAB], oy)

    halves = []
    for half in range(2):
        pairs = [received(64 * (4 * half + c), 64) for c in range(4)]
        own = [own_ref[pl.ds(64 * (4 * half + c), 64), :] for c in range(4)]
        lower = [line[4 * half + c][:64] for c in range(4)]
        upper = [line[4 * half + c][64:] for c in range(4)]
        merged = over(own, over(upper, [above for _, above in pairs]))
        halves.append(over([below for below, _ in pairs], over(lower, merged)))
    for c in range(4):
        low, high = halves[0][c], halves[1][c]
        low_turned, high_turned = pltpu.roll(low, 64, 1), pltpu.roll(high, 64, 1)
        mine_ref[c] = jnp.where(lane < 64, low_turned, high_turned)
        left = jnp.where(lane < 64, low[:32], low_turned[32:])
        right = jnp.where(lane < 64, high_turned[:32], high[32:])
        near_out_ref[pl.ds(32 * c, 32), :] = jnp.where(odd_col, left, right)
        far_out_ref[pl.ds(32 * c, 32), :] = jnp.where(odd_col, right, left)

    below_col, above_col = received(576, 64)
    negative = jnp.concatenate([fvec_ref[3:4, 0:SLAB]] * 2, axis=1) < 0.0
    pair = jnp.concatenate(
        [jnp.where(negative, cols_ref[...], above_col), jnp.where(negative, below_col, cols_ref[...])], axis=0
    )

    def amount(z):
        offset = shift_ref[0, z % SLAB]
        return jnp.where(offset < 0, offset + COLS, offset + 64)

    here = turn_rows(jnp.transpose(pair), amount)
    columns = here + jnp.concatenate([fy, fy], axis=0) * (pltpu.roll(here, 1, 1) - here)
    u_ref[...] = columns
    turned = pltpu.roll(columns, 64, 1)
    last = jnp.where(lane < 64, columns[:32], turned[32:64])
    first = jnp.where(lane < 64, columns[64:96], turned[96:])
    near_out_ref[pl.ds(128, 32), :] = jnp.where(odd_col, first, last)
    far_out_ref[pl.ds(128, 32), :] = jnp.where(odd_col, last, first)


def columns_kernel(scale, limit, edge_ref, mine_ref, near_ref, far_ref, u_ref, zrow_ref, zcol_ref, fvec_ref, fcol_ref, out_ref):
    lane = lax.broadcasted_iota(jnp.int32, (1, COLS), 1)
    odd_col = edge_ref[1] == 1
    fx, rate, oy, ox = fcol_ref[:, 1:2], fcol_ref[:, 2:3] * scale, fcol_ref[:, 3:4], fcol_ref[:, 4:5]

    def received(start, size):
        near, far = near_ref[pl.ds(start, size), :], far_ref[pl.ds(start, size), :]
        return jnp.where(odd_col, far, near), jnp.where(odd_col, near, far)

    right_first, left_last = [
        jnp.concatenate([part, pltpu.roll(part, 64, 1)], axis=0) for part in received(128, 32)
    ]
    here = jnp.where(ox < 0.0, right_first, u_ref[pl.ds(64, 64), :])
    behind = jnp.where(ox < 0.0, u_ref[pl.ds(0, 64), :], left_last)
    sheared = here + fx * (behind - here)
    row = (lane + edge_ref[2]).astype(jnp.float32) - oy
    optical = jnp.where((row >= 0.0) & (row <= limit), rate * softplus(sheared), 0.0)
    line = line_composite(sheared, [optical], fvec_ref[4:5, 0:SLAB], ox)
    line = [pltpu.roll(jnp.transpose(part)[:64], 64, 1) for part in line]

    front, behind = [], []
    for c in range(4):
        right, left = received(32 * c, 32)
        upper = jnp.concatenate([pltpu.roll(right, 64, 1), right], axis=0)
        lower = jnp.concatenate([left, pltpu.roll(left, 64, 1)], axis=0)
        own = mine_ref[c]
        front.append(jnp.where(lane < 64, own, upper))
        behind.append(jnp.where(lane < 64, lower, own))
    inner = over(front, over(line, behind))
    total = jnp.sum(fvec_ref[2:3, :], axis=1, keepdims=True)
    pre = jnp.maximum(zrow_ref[:, 0:1], zcol_ref[0:1, :])
    post = jnp.minimum(jnp.maximum(zrow_ref[:, 1:2], zcol_ref[1:2, :]), total - pre)
    flat = []
    for amount in (pre, jnp.maximum(post, 0.0)):
        fade = 1.0 - jnp.exp((-scale * LN2) * amount)
        flat.append([jnp.zeros_like(fade), fade, math.tanh(0.4) * fade, fade])
    whole = over(flat[0], over(inner, flat[1]))
    pieces = out_ref.shape[0]
    height = ROWS // pieces
    for p in range(pieces):
        for c in range(4):
            out_ref[p, c] = whole[c][p * height : (p + 1) * height]


def fold_kernel(in_ref, out_ref):
    merged = channels(in_ref, 0)
    for slab in range(1, in_ref.shape[0]):
        merged = over(merged, channels(in_ref, slab))
    out_ref[0] = 0.5 * (merged[3] + merged[0])
    out_ref[1] = merged[1]
    out_ref[2] = 0.5 * (merged[3] + merged[2])
    out_ref[3] = merged[3]


def matching(count, first):
    pairs = [(i, i + 1) for i in range(first, count - 1, 2)]
    return pairs + [(j, i) for i, j in pairs]


def body(coefficients, shifts, fraction, absorb):
    depth_count = lax.axis_size("depth")
    row_count = lax.axis_size("imgy")
    col_count = lax.axis_size("imgx")
    scale = 2.0 / (SLAB * depth_count)
    iy, ix = lax.axis_index("imgy"), lax.axis_index("imgx")

    shift_rows, shift_cols = shifts[0], shifts[1]
    edge = jnp.stack([iy % 2, ix % 2, iy * ROWS]).astype(jnp.int32)
    lines = jnp.concatenate([fraction, absorb[None], shifts.astype(jnp.float32)], axis=0)
    vectors = jnp.pad(lines, ((0, 3), (0, COLS - SLAB)))
    columns = jnp.pad(lines.T, ((0, 0), (0, 3)))

    sent = f32(640, COLS)
    near, own, far, row_planes, col_planes = call(
        functools.partial(tile_kernel, scale),
        (sent, f32(512, COLS), sent, f32(128, COLS), f32(64, COLS)),
        [SMEM_SPEC] + [HBM_SPEC] * 4,
        [
            pltpu.SMEM((2, SLAB), jnp.int32),
            pltpu.SMEM((2, SLAB), jnp.float32),
            pltpu.SMEM((SLAB,), jnp.float32),
            pltpu.VMEM((SLAB, ROWS, COLS), jnp.float32),
            pltpu.VMEM((16, 16, COLS), jnp.float32),
            pltpu.VMEM((32, 32, COLS), jnp.float32),
            pltpu.VMEM((64, 64, COLS), jnp.float32),
            pltpu.VMEM((64, COLS), jnp.float32),
            pltpu.VMEM((8, EXT, COLS), jnp.float32),
            pltpu.SemaphoreType.DMA((7,)),
        ],
        flops=300_000_000,
        bytes_moved=4 << 20,
    )(edge, *[pltpu.with_memory_space_constraint(a, pltpu.HBM) for a in (shifts, fraction, absorb, coefficients)])

    far = lax.ppermute(far, "imgy", matching(row_count, 1))
    near = lax.ppermute(near, "imgy", matching(row_count, 0))
    packed = f32(160, COLS)
    mine, near, far, sheared_cols = call(
        functools.partial(rows_kernel, scale),
        (f32(4, ROWS, COLS), packed, packed, f32(128, COLS)),
        [SMEM_SPEC] * 2 + [VMEM_SPEC] * 7,
    )(shifts, edge, own, near, far, row_planes, col_planes, vectors, columns)
    far = lax.ppermute(far, "imgx", matching(col_count, 1))
    near = lax.ppermute(near, "imgx", matching(col_count, 0))

    image_rows = iy * ROWS + jnp.arange(ROWS, dtype=jnp.int32)
    image_cols = ix * COLS + jnp.arange(COLS, dtype=jnp.int32)

    def outside(pixels, offsets, limit):
        position = pixels[:, None] - offsets[None, :]
        pre = jnp.sum(jnp.where(position > limit, absorb[None, :], 0.0), axis=1)
        post = jnp.sum(jnp.where(position < 0, absorb[None, :], 0.0), axis=1)
        return pre, post

    zrow = jnp.stack(outside(image_rows, shift_rows, ROWS * row_count), axis=1)
    zcol = jnp.stack(outside(image_cols, shift_cols, COLS * col_count), axis=0)
    pieces = call(
        functools.partial(columns_kernel, scale, float(ROWS * row_count)),
        f32(depth_count, 4, ROWS // depth_count, COLS),
        [SMEM_SPEC] + [VMEM_SPEC] * 8,
    )(edge, mine, near, far, sheared_cols, zrow, zcol, vectors, columns)
    incoming = lax.all_to_all(pieces, "depth", split_axis=0, concat_axis=0, tiled=True)
    image = call(fold_kernel, f32(4, ROWS // depth_count, COLS), [VMEM_SPEC])(incoming)
    return image[:, None]


def solution(mesh):
    in_specs = (P("depth", "imgy", "imgx"), P(None, "depth"), P(None, "depth"), P("depth"))
    out_specs = P(None, "imgy", "depth", "imgx")
    return jax.shard_map(body, mesh=mesh, in_specs=in_specs, out_specs=out_specs, check_vma=False)
```

```python
import functools
import math

import jax
import jax.numpy as jnp
from jax import lax
from jax.experimental import pallas as pl
from jax.experimental.pallas import tpu as pltpu
from jax.sharding import PartitionSpec as P

BRICK = 64
SLAB = 64
ROWS = 64
COLS = 128
EXT = 208
SLICE_UNROLL = 16
LN2 = math.log(2.0)
LOG2E = 1.0 / math.log(2.0)
VMEM_SPEC = pl.BlockSpec(memory_space=pltpu.VMEM)
SMEM_SPEC = pl.BlockSpec(memory_space=pltpu.SMEM)
HBM_SPEC = pl.BlockSpec(memory_space=pltpu.HBM)
CHUNK = 16
INTERPRET = False


def call(kernel, out_shape, in_specs, scratch=(), flops=1000, bytes_moved=1000):
    specs = jax.tree.map(lambda _: VMEM_SPEC, out_shape)
    return pl.pallas_call(
        kernel,
        out_shape=out_shape,
        in_specs=in_specs,
        out_specs=specs,
        scratch_shapes=list(scratch),
        interpret=INTERPRET,
        compiler_params=pltpu.CompilerParams(vmem_limit_bytes=24 << 20),
        cost_estimate=pl.CostEstimate(flops=flops, bytes_accessed=bytes_moved, transcendentals=0),
    )


def f32(*shape):
    return jax.ShapeDtypeStruct(shape, jnp.float32)


def lane_table(half):
    source = lax.broadcasted_iota(jnp.int32, (2 * COLS, COLS), 0) % COLS
    target = lax.broadcasted_iota(jnp.int32, (2 * COLS, COLS), 1)
    local = target % BRICK
    start = target - local
    pair = local // 2
    weight = jnp.where(local % 2 == 1, 0.5, -0.5)
    inside = local < 2 * half
    low = jnp.where(inside & (source == start + pair), 1.0, 0.0)
    high = jnp.where(inside & (source == start + half + pair), weight, 0.0)
    return (low + high).astype(jnp.bfloat16)


def lane_lift(block, table):
    coarse = block.astype(jnp.bfloat16)
    rest = (block - coarse.astype(jnp.float32)).astype(jnp.bfloat16)
    both = jnp.concatenate([coarse, rest], axis=1)
    return jnp.dot(both, table, preferred_element_type=jnp.float32)


def softplus(sheared):
    return jnp.maximum(sheared, 0.0) + jnp.log(1.0 + jnp.exp(-jnp.abs(sheared)))


def tint(sheared):
    return jnp.tanh(0.75 * sheared), jnp.exp(-0.5 * (sheared * sheared)), jnp.tanh(0.4 - 0.5 * sheared)


def tile_kernel(
    scale, edge_ref, shift_hbm, frac_hbm, absorb_hbm, c_hbm, near_ref, own_ref, far_ref, rows_ref, cols_ref,
    shift_ref, frac_ref, absorb_ref, c_ref, s2_ref, s1_ref, d_ref, plane_ref, acc_ref, sems,
):
    def load(index, planes, rows):
        block = (pl.ds(*planes), pl.ds(*rows))
        return pltpu.make_async_copy(c_hbm.at[block], c_ref.at[block], sems.at[index])

    loads = [load(0, (0, 16), (0, 16)), load(1, (16, 16), (0, 32)), load(2, (0, 16), (16, 16))]
    loads += [load(3, (0, 16), (32, 32)), load(4, (32, 16), (0, 64)), load(5, (16, 16), (32, 32)), load(6, (48, 16), (0, 64))]
    scalars = [
        pltpu.make_async_copy(shift_hbm, shift_ref, sems.at[7]),
        pltpu.make_async_copy(frac_hbm, frac_ref, sems.at[8]),
        pltpu.make_async_copy(absorb_hbm, absorb_ref, sems.at[9]),
    ]
    for copy in loads + scalars:
        copy.start()
    for index in range(8):
        acc_ref[index] = jnp.full((EXT, COLS), 1.0 if index % 4 == 3 else 0.0, jnp.float32)

    lane = lax.broadcasted_iota(jnp.int32, (1, COLS), 1)
    sub = lax.broadcasted_iota(jnp.int32, (8, COLS), 0)

    def level(half, below, out_ref, on_result, init, unroll, span=None):
        table = lane_table(half)

        def step(i, carry):
            if below is None:
                low = c_ref[i, : 2 * half, :]
            else:
                corner = jnp.where(lane % BRICK < half, below[i], c_ref[i, :half, :])
                low = jnp.concatenate([corner, c_ref[i, half : 2 * half, :]], axis=0)
            high = c_ref[i + half, : 2 * half, :]
            planes = []
            even = low - 0.5 * high
            for part in (even, even + high):
                row_even = part[:half] - 0.5 * part[half:]
                planes += [row_even, row_even + part[half:]]
            result = lane_lift(jnp.concatenate(planes, axis=0), table)
            for odd in range(2):
                for row_odd in range(2):
                    start = (2 * odd + row_odd) * half
                    out_ref[2 * i + odd, pl.ds(row_odd, half, stride=2), :] = result[start : start + half]
            return on_result(i, result, carry)

        first, last = span or (0, half)
        return lax.fori_loop(first, last, step, init, unroll=unroll)

    def ignore(i, result, carry):
        return carry

    def boundary(i, result, plane):
        for odd in range(2):
            z = 2 * i + odd
            piece = result[64 * odd : 64 * odd + 64]
            rows_ref[pl.ds(z, 1), :] = piece[63:64]
            rows_ref[pl.ds(64 + z, 1), :] = piece[0:1]
            plane = jnp.where(lane // 2 == z, pltpu.roll(piece, 2 * z + 1, 1), plane)
        return plane

    loads[0].wait()
    level(8, None, s2_ref, ignore, 0, 8)
    loads[1].wait()
    loads[2].wait()
    level(16, s2_ref, s1_ref, ignore, 0, 16)
    loads[3].wait()
    loads[4].wait()
    plane = level(32, s1_ref, d_ref, boundary, jnp.zeros((64, COLS), jnp.float32), 16, (0, 16))
    loads[5].wait()
    loads[6].wait()
    plane_ref[...] = level(32, s1_ref, d_ref, boundary, plane, 16, (16, 32))
    for row_odd in range(2):
        cols_ref[pl.ds(row_odd, 32, stride=2), :] = plane_ref[pl.ds(32 * row_odd, 32), :]

    for copy in scalars:
        copy.wait()

    inside = lax.broadcasted_iota(jnp.int32, (ROWS, COLS), 0) > 0

    def slice_step(z, carry):
        k = shift_ref[1, z] + 64
        here = d_ref[z]
        behind = jnp.concatenate([pltpu.roll(d_ref[z, 0:8, :], 1, 0), d_ref[z, 7:63, :]], axis=0)
        mixed = here + frac_ref[0, z] * (behind - here)
        left = pltpu.roll(mixed, 1, 1)
        sheared = pltpu.roll(mixed + frac_ref[1, z] * (left - mixed), k, 1)
        twos = LOG2E * sheared
        positive = jnp.maximum(twos, 0.0)
        soft = positive + jnp.log2(1.0 + jnp.exp2((twos - positive) - positive))
        keep = jnp.exp2((-absorb_ref[z] * scale) * soft)
        tints = jnp.tanh(0.75 * sheared), jnp.exp2((-0.5 * twos) * sheared), jnp.tanh(0.4 - 0.5 * sheared)
        view = acc_ref.at[:, pl.ds(shift_ref[0, z] + 64, 64), :]
        right = lane < k
        value = [jnp.where(right, view[4 + c], view[c]) for c in range(4)]
        after = value[3] * keep
        weight = value[3] - after
        value = [value[c] + weight * tints[c] for c in range(3)] + [after]
        for c in range(4):
            pltpu.store(view.at[c], value[c], mask=inside & (lane > k))
            pltpu.store(view.at[4 + c], value[c], mask=inside & right)
        return carry

    lax.fori_loop(0, SLAB, slice_step, 0, unroll=SLICE_UNROLL)

    odd = edge_ref[0]
    for start, out_ref in ((128 - 128 * odd, near_ref), (64, own_ref), (128 * odd, far_ref)):
        for half in range(2):
            for channel in range(4):
                value = acc_ref[4 * half + channel, pl.ds(pl.multiple_of(start, 64), 64), :]
                value = 1.0 - value if channel == 3 else value
                out_ref[pl.ds(64 * (4 * half + channel), 64), :] = value
    near_ref[pl.ds(512, 64), :] = rows_ref[pl.ds(pl.multiple_of(64 * odd, 64), 64), :]
    far_ref[pl.ds(512, 64), :] = rows_ref[pl.ds(pl.multiple_of(64 - 64 * odd, 64), 64), :]
    near_ref[pl.ds(576, 64), :] = cols_ref[...]
    far_ref[pl.ds(576, 64), :] = cols_ref[...]


def over(front, behind):
    through = 1.0 - front[3]
    return [front[c] + through * behind[c] for c in range(4)]


def channels(ref, *index):
    return [ref[(*index, c)] for c in range(4)]


def turn_rows(plane, amounts):
    sub = lax.broadcasted_iota(jnp.int32, (8, COLS), 0)
    tiles = []
    for t in range(plane.shape[0] // 8):
        tile = plane[8 * t : 8 * t + 8]
        turned = pltpu.roll(tile, amounts(8 * t), 1)
        for r in range(1, 8):
            turned = jnp.where(sub == r, pltpu.roll(tile, amounts(8 * t + r), 1), turned)
        tiles.append(turned)
    return jnp.concatenate(tiles, axis=0)


def select_dot(chosen, values):
    coarse = values.astype(jnp.bfloat16)
    rest = values - coarse.astype(jnp.float32)
    fine = rest.astype(jnp.bfloat16)
    left = chosen.astype(jnp.bfloat16)
    return jnp.dot(left, coarse, preferred_element_type=jnp.float32) + jnp.dot(
        left, fine, preferred_element_type=jnp.float32
    )


def line_composite(sheared, opticals, key_row, key_col):
    first = lax.broadcasted_iota(jnp.int32, (SLAB, SLAB), 0)
    second = lax.broadcasted_iota(jnp.int32, (SLAB, SLAB), 1)
    ahead = jnp.where((second < first) & (key_row == key_col), 1.0, 0.0)
    target = lax.broadcasted_iota(jnp.int32, (2 * SLAB, SLAB), 0).astype(jnp.float32)
    chosen = jnp.where(target == key_row + 64.0, 1.0, 0.0)
    before = select_dot(ahead, jnp.concatenate(opticals, axis=1))
    tints = tint(sheared)
    pieces = []
    for half, optical in enumerate(opticals):
        front = before[:, COLS * half : COLS * half + COLS]
        weight = jnp.exp(-front) - jnp.exp(-(front + optical))
        pieces += [weight * tints[0], weight * tints[1], weight * tints[2], weight]
    total = select_dot(chosen, jnp.concatenate(pieces, axis=1))
    return [total[:, COLS * p : COLS * p + COLS] for p in range(len(pieces))]


def rows_kernel(
    scale, shift_ref, edge_ref, own_ref, near_ref, far_ref, rows_ref, cols_ref, fvec_ref, fcol_ref, fy_ref,
    mine_ref, near_out_ref, far_out_ref, u_ref,
):
    lane = lax.broadcasted_iota(jnp.int32, (1, COLS), 1)
    odd_row, odd_col = edge_ref[0] == 1, edge_ref[1] == 1
    fy, fx, rate = fcol_ref[:, 0:1], fcol_ref[:, 1:2], fcol_ref[:, 2:3] * scale
    oy, ox = fcol_ref[:, 3:4], fcol_ref[:, 4:5]

    def received(start, size):
        near, far = near_ref[pl.ds(start, size), :], far_ref[pl.ds(start, size), :]
        return jnp.where(odd_row, far, near), jnp.where(odd_row, near, far)

    below_row, above_row = received(512, 64)
    here = jnp.where(oy < 0.0, below_row, rows_ref[pl.ds(64, 64), :])
    behind = jnp.where(oy < 0.0, rows_ref[pl.ds(0, 64), :], above_row)
    mixed = here + fy * (behind - here)
    sheared = mixed + fx * (pltpu.roll(mixed, 1, 1) - mixed)
    sheared = turn_rows(sheared, lambda z: shift_ref[1, z] + 64)
    optical = rate * softplus(sheared)
    place = lane.astype(jnp.float32)
    opticals = [jnp.where(place > ox + 64.0, optical, 0.0), jnp.where(place < ox + 64.0, optical, 0.0)]
    line = line_composite(sheared, opticals, fvec_ref[3:4, 0:SLAB], oy)

    halves = []
    for half in range(2):
        pairs = [received(64 * (4 * half + c), 64) for c in range(4)]
        own = [own_ref[pl.ds(64 * (4 * half + c), 64), :] for c in range(4)]
        lower = [line[4 * half + c][:64] for c in range(4)]
        upper = [line[4 * half + c][64:] for c in range(4)]
        merged = over(own, over(upper, [above for _, above in pairs]))
        halves.append(over([below for below, _ in pairs], over(lower, merged)))
    for c in range(4):
        low, high = halves[0][c], halves[1][c]
        low_turned, high_turned = pltpu.roll(low, 64, 1), pltpu.roll(high, 64, 1)
        mine_ref[c] = jnp.where(lane < 64, low_turned, high_turned)
        left = jnp.where(lane < 64, low[:32], low_turned[32:])
        right = jnp.where(lane < 64, high_turned[:32], high[32:])
        near_out_ref[pl.ds(32 * c, 32), :] = jnp.where(odd_col, left, right)
        far_out_ref[pl.ds(32 * c, 32), :] = jnp.where(odd_col, right, left)

    below_col, above_col = received(576, 64)
    negative = fvec_ref[5:6, :] < 0.0
    pair = jnp.concatenate(
        [jnp.where(negative, cols_ref[...], above_col), jnp.where(negative, below_col, cols_ref[...])], axis=0
    )

    def amount(z):
        offset = shift_ref[0, z // 2]
        return jnp.where(offset < 0, offset + COLS, offset + 64)

    here = turn_rows(jnp.transpose(pair), amount)
    u_ref[...] = here + fy_ref[:, 0:1] * (pltpu.roll(here, 1, 1) - here)

    def pack(column):
        upper = u_ref[pl.ds(column, 32, stride=2), :]
        return jnp.where(lane < 64, upper, pltpu.roll(u_ref[pl.ds(64 + column, 32, stride=2), :], 64, 1))

    last, first = pack(0), pack(1)
    near_out_ref[pl.ds(128, 32), :] = jnp.where(odd_col, first, last)
    far_out_ref[pl.ds(128, 32), :] = jnp.where(odd_col, last, first)


def columns_kernel(scale, limit, edge_ref, mine_ref, near_ref, far_ref, u_ref, zrow_ref, zcol_ref, fvec_ref, fcol_ref, out_ref):
    lane = lax.broadcasted_iota(jnp.int32, (1, COLS), 1)
    odd_col = edge_ref[1] == 1
    fx, rate, oy, ox = fcol_ref[:, 1:2], fcol_ref[:, 2:3] * scale, fcol_ref[:, 3:4], fcol_ref[:, 4:5]

    def received(start, size):
        near, far = near_ref[pl.ds(start, size), :], far_ref[pl.ds(start, size), :]
        return jnp.where(odd_col, far, near), jnp.where(odd_col, near, far)

    right_first, left_last = [
        jnp.concatenate([part, pltpu.roll(part, 64, 1)], axis=0) for part in received(128, 32)
    ]
    here = jnp.where(ox < 0.0, right_first, u_ref[pl.ds(1, 64, stride=2), :])
    behind = jnp.where(ox < 0.0, u_ref[pl.ds(0, 64, stride=2), :], left_last)
    sheared = here + fx * (behind - here)
    row = (lane + edge_ref[2]).astype(jnp.float32) - oy
    optical = jnp.where((row >= 0.0) & (row <= limit), rate * softplus(sheared), 0.0)
    line = line_composite(sheared, [optical], fvec_ref[4:5, 0:SLAB], ox)
    line = [pltpu.roll(jnp.transpose(part)[:64], 64, 1) for part in line]

    front, behind = [], []
    for c in range(4):
        right, left = received(32 * c, 32)
        upper = jnp.concatenate([pltpu.roll(right, 64, 1), right], axis=0)
        lower = jnp.concatenate([left, pltpu.roll(left, 64, 1)], axis=0)
        own = mine_ref[c]
        front.append(jnp.where(lane < 64, own, upper))
        behind.append(jnp.where(lane < 64, lower, own))
    inner = over(front, over(line, behind))
    total = jnp.sum(fvec_ref[2:3, :], axis=1, keepdims=True)
    pre = jnp.maximum(zrow_ref[:, 0:1], zcol_ref[0:1, :])
    post = jnp.minimum(jnp.maximum(zrow_ref[:, 1:2], zcol_ref[1:2, :]), total - pre)
    flat = []
    for amount in (pre, jnp.maximum(post, 0.0)):
        fade = 1.0 - jnp.exp((-scale * LN2) * amount)
        flat.append([jnp.zeros_like(fade), fade, math.tanh(0.4) * fade, fade])
    whole = over(flat[0], over(inner, flat[1]))
    pieces = out_ref.shape[0]
    height = ROWS // pieces
    for p in range(pieces):
        for c in range(4):
            out_ref[p, c] = whole[c][p * height : (p + 1) * height]


def fold_kernel(in_ref, out_ref):
    merged = channels(in_ref, 0)
    for slab in range(1, in_ref.shape[0]):
        merged = over(merged, channels(in_ref, slab))
    out_ref[0] = 0.5 * (merged[3] + merged[0])
    out_ref[1] = merged[1]
    out_ref[2] = 0.5 * (merged[3] + merged[2])
    out_ref[3] = merged[3]


def tile_scratch():
    return [
        pltpu.SMEM((2, SLAB), jnp.int32),
        pltpu.SMEM((2, SLAB), jnp.float32),
        pltpu.SMEM((SLAB,), jnp.float32),
        pltpu.VMEM((SLAB, ROWS, COLS), jnp.float32),
        pltpu.VMEM((16, 16, COLS), jnp.float32),
        pltpu.VMEM((32, 32, COLS), jnp.float32),
        pltpu.VMEM((64, 64, COLS), jnp.float32),
        pltpu.VMEM((64, COLS), jnp.float32),
        pltpu.VMEM((8, EXT, COLS), jnp.float32),
        pltpu.SemaphoreType.DMA((10,)),
    ]


def matching(count, first):
    pairs = [(i, i + 1) for i in range(first, count - 1, 2)]
    return pairs + [(j, i) for i, j in pairs]


def body(coefficients, shifts, fraction, absorb):
    depth_count = lax.axis_size("depth")
    row_count = lax.axis_size("imgy")
    col_count = lax.axis_size("imgx")
    scale = 2.0 / (SLAB * depth_count)
    iy, ix = lax.axis_index("imgy"), lax.axis_index("imgx")

    shift_rows, shift_cols = shifts[0], shifts[1]
    edge = jnp.stack([iy % 2, ix % 2, iy * ROWS]).astype(jnp.int32)
    lines = jnp.concatenate([fraction, absorb[None], shifts.astype(jnp.float32)], axis=0)
    twice = jnp.repeat(lines[3:4], 2, axis=1)
    vectors = jnp.concatenate([jnp.pad(lines, ((0, 0), (0, COLS - SLAB))), twice, jnp.zeros((2, COLS))], axis=0)
    fy_twice = jnp.repeat(fraction[0], 2)[:, None]
    columns = jnp.pad(lines.T, ((0, 0), (0, 3)))

    sent = f32(640, COLS)
    near, own, far, row_planes, col_planes = call(
        functools.partial(tile_kernel, scale),
        (sent, f32(512, COLS), sent, f32(128, COLS), f32(64, COLS)),
        [SMEM_SPEC] + [HBM_SPEC] * 4,
        tile_scratch(),
        flops=300_000_000,
        bytes_moved=4 << 20,
    )(edge, *[pltpu.with_memory_space_constraint(a, pltpu.HBM) for a in (shifts, fraction, absorb, coefficients)])

    far = lax.ppermute(far, "imgy", matching(row_count, 1))
    near = lax.ppermute(near, "imgy", matching(row_count, 0))
    packed = f32(160, COLS)
    mine, near, far, sheared_cols = call(
        functools.partial(rows_kernel, scale),
        (f32(4, ROWS, COLS), packed, packed, f32(128, COLS)),
        [SMEM_SPEC] * 2 + [VMEM_SPEC] * 8,
    )(shifts, edge, own, near, far, row_planes, col_planes, vectors, columns, fy_twice)
    far = lax.ppermute(far, "imgx", matching(col_count, 1))
    near = lax.ppermute(near, "imgx", matching(col_count, 0))

    image_rows = iy * ROWS + jnp.arange(ROWS, dtype=jnp.int32)
    image_cols = ix * COLS + jnp.arange(COLS, dtype=jnp.int32)

    def outside(pixels, offsets, limit):
        position = pixels[:, None] - offsets[None, :]
        pre = jnp.sum(jnp.where(position > limit, absorb[None, :], 0.0), axis=1)
        post = jnp.sum(jnp.where(position < 0, absorb[None, :], 0.0), axis=1)
        return pre, post

    zrow = jnp.stack(outside(image_rows, shift_rows, ROWS * row_count), axis=1)
    zcol = jnp.stack(outside(image_cols, shift_cols, COLS * col_count), axis=0)
    pieces = call(
        functools.partial(columns_kernel, scale, float(ROWS * row_count)),
        f32(depth_count, 4, ROWS // depth_count, COLS),
        [SMEM_SPEC] + [VMEM_SPEC] * 8,
    )(edge, mine, near, far, sheared_cols, zrow, zcol, vectors, columns)
    incoming = lax.all_to_all(pieces, "depth", split_axis=0, concat_axis=0, tiled=True)
    image = call(fold_kernel, f32(4, ROWS // depth_count, COLS), [VMEM_SPEC])(incoming)
    return image[:, None]


def solution(mesh):
    in_specs = (P("depth", "imgy", "imgx"), P(None, "depth"), P(None, "depth"), P("depth"))
    out_specs = P(None, "imgy", "depth", "imgx")
    return jax.shard_map(body, mesh=mesh, in_specs=in_specs, out_specs=out_specs, check_vma=False)
```

```python
import functools
import math

import jax
import jax.numpy as jnp
from jax import lax
from jax.experimental import pallas as pl
from jax.experimental.pallas import tpu as pltpu
from jax.sharding import PartitionSpec as P


BRICK = 64
SLAB = 64
ROWS = 64
COLS = 128
EXT = 208
SLICE_UNROLL = 16
LN2 = math.log(2.0)
LOG2E = 1.0 / math.log(2.0)
VMEM_SPEC = pl.BlockSpec(memory_space=pltpu.VMEM)
SMEM_SPEC = pl.BlockSpec(memory_space=pltpu.SMEM)
HBM_SPEC = pl.BlockSpec(memory_space=pltpu.HBM)
INTERPRET = False


def call(kernel, out_shape, in_specs, scratch=(), flops=1000, bytes_moved=1000):
    specs = jax.tree.map(lambda _: VMEM_SPEC, out_shape)
    return pl.pallas_call(
        kernel,
        out_shape=out_shape,
        in_specs=in_specs,
        out_specs=specs,
        scratch_shapes=list(scratch),
        interpret=INTERPRET,
        compiler_params=pltpu.CompilerParams(vmem_limit_bytes=24 << 20),
        cost_estimate=pl.CostEstimate(flops=flops, bytes_accessed=bytes_moved, transcendentals=0),
    )


def f32(*shape):
    return jax.ShapeDtypeStruct(shape, jnp.float32)


def lane_table(half):
    source = lax.broadcasted_iota(jnp.int32, (2 * COLS, COLS), 0) % COLS
    target = lax.broadcasted_iota(jnp.int32, (2 * COLS, COLS), 1)
    local = target % BRICK
    start = target - local
    pair = local // 2
    weight = jnp.where(local % 2 == 1, 0.5, -0.5)
    inside = local < 2 * half
    low = jnp.where(inside & (source == start + pair), 1.0, 0.0)
    high = jnp.where(inside & (source == start + half + pair), weight, 0.0)
    return (low + high).astype(jnp.bfloat16)


def lane_lift(block, table):
    coarse = block.astype(jnp.bfloat16)
    rest = (block - coarse.astype(jnp.float32)).astype(jnp.bfloat16)
    both = jnp.concatenate([coarse, rest], axis=1)
    return jnp.dot(both, table, preferred_element_type=jnp.float32)


def softplus(sheared):
    return jnp.maximum(sheared, 0.0) + jnp.log(1.0 + jnp.exp(-jnp.abs(sheared)))


def tint(sheared):
    return jnp.tanh(0.75 * sheared), jnp.exp(-0.5 * (sheared * sheared)), jnp.tanh(0.4 - 0.5 * sheared)


def tile_kernel(
    scale, edge_ref, shift_hbm, frac_hbm, absorb_hbm, c_hbm, near_ref, own_ref, far_ref, rows_ref, cols_ref,
    shift_ref, frac_ref, absorb_ref, c_ref, s2_ref, s1_ref, d_ref, plane_ref, acc_ref, sems,
):
    def load(index, planes, rows):
        block = (pl.ds(*planes), pl.ds(*rows))
        return pltpu.make_async_copy(c_hbm.at[block], c_ref.at[block], sems.at[index])

    loads = [load(0, (0, 16), (0, 16)), load(1, (16, 16), (0, 32)), load(2, (0, 16), (16, 16))]
    loads += [load(3, (0, 16), (32, 32)), load(4, (32, 16), (0, 64)), load(5, (16, 16), (32, 32)), load(6, (48, 16), (0, 64))]
    scalars = [
        pltpu.make_async_copy(shift_hbm, shift_ref, sems.at[7]),
        pltpu.make_async_copy(frac_hbm, frac_ref, sems.at[8]),
        pltpu.make_async_copy(absorb_hbm, absorb_ref, sems.at[9]),
    ]
    for copy in loads + scalars:
        copy.start()
    for index in range(8):
        acc_ref[index] = jnp.full((EXT, COLS), 1.0 if index % 4 == 3 else 0.0, jnp.float32)

    lane = lax.broadcasted_iota(jnp.int32, (1, COLS), 1)
    sub = lax.broadcasted_iota(jnp.int32, (8, COLS), 0)

    tables = {half: lane_table(half) for half in (8, 16, 32)}

    def level(half, below, out_ref, on_result, init, unroll, span=None):
        table = tables[half]

        def step(i, carry):
            if below is None:
                low = c_ref[i, : 2 * half, :]
            else:
                corner = jnp.where(lane % BRICK < half, below[i], c_ref[i, :half, :])
                low = jnp.concatenate([corner, c_ref[i, half : 2 * half, :]], axis=0)
            high = c_ref[i + half, : 2 * half, :]
            planes = []
            even = low - 0.5 * high
            for part in (even, even + high):
                row_even = part[:half] - 0.5 * part[half:]
                planes += [row_even, row_even + part[half:]]
            result = lane_lift(jnp.concatenate(planes, axis=0), table)
            for odd in range(2):
                for row_odd in range(2):
                    start = (2 * odd + row_odd) * half
                    out_ref[2 * i + odd, pl.ds(row_odd, half, stride=2), :] = result[start : start + half]
            return on_result(i, result, carry)

        first, last = span or (0, half)
        return lax.fori_loop(first, last, step, init, unroll=unroll)

    def ignore(i, result, carry):
        return carry

    def boundary(i, result, plane):
        for odd in range(2):
            z = 2 * i + odd
            piece = result[64 * odd : 64 * odd + 64]
            rows_ref[pl.ds(z, 1), :] = piece[63:64]
            rows_ref[pl.ds(64 + z, 1), :] = piece[0:1]
            plane = jnp.where(lane // 2 == z, pltpu.roll(piece, 2 * z + 1, 1), plane)
        return plane

    loads[0].wait()
    level(8, None, s2_ref, ignore, 0, 8)
    loads[1].wait()
    loads[2].wait()
    level(16, s2_ref, s1_ref, ignore, 0, 16)
    loads[3].wait()
    loads[4].wait()
    plane = level(32, s1_ref, d_ref, boundary, jnp.zeros((64, COLS), jnp.float32), 16, (0, 16))
    loads[5].wait()
    loads[6].wait()
    plane_ref[...] = level(32, s1_ref, d_ref, boundary, plane, 16, (16, 32))
    for row_odd in range(2):
        cols_ref[pl.ds(row_odd, 32, stride=2), :] = plane_ref[pl.ds(32 * row_odd, 32), :]

    for copy in scalars:
        copy.wait()

    inside = lax.broadcasted_iota(jnp.int32, (ROWS, COLS), 0) > 0

    def slice_step(z, carry):
        k = shift_ref[1, z] + 64
        here = d_ref[z]
        behind = jnp.concatenate([pltpu.roll(d_ref[z, 0:8, :], 1, 0), d_ref[z, 7:63, :]], axis=0)
        mixed = here + frac_ref[0, z] * (behind - here)
        left = pltpu.roll(mixed, 1, 1)
        sheared = pltpu.roll(mixed + frac_ref[1, z] * (left - mixed), k, 1)
        twos = LOG2E * sheared
        positive = jnp.maximum(twos, 0.0)
        soft = positive + jnp.log2(1.0 + jnp.exp2((twos - positive) - positive))
        keep = jnp.exp2((-absorb_ref[z] * scale) * soft)
        tints = jnp.tanh(0.75 * sheared), jnp.exp2((-0.5 * twos) * sheared), jnp.tanh(0.4 - 0.5 * sheared)
        view = acc_ref.at[:, pl.ds(shift_ref[0, z] + 64, 64), :]
        right = lane < k
        value = [jnp.where(right, view[4 + c], view[c]) for c in range(4)]
        after = value[3] * keep
        weight = value[3] - after
        value = [value[c] + weight * tints[c] for c in range(3)] + [after]
        for c in range(4):
            pltpu.store(view.at[c], value[c], mask=inside & (lane > k))
            pltpu.store(view.at[4 + c], value[c], mask=inside & right)
        return carry

    lax.fori_loop(0, SLAB, slice_step, 0, unroll=SLICE_UNROLL)

    odd = edge_ref[0]
    for start, out_ref in ((128 - 128 * odd, near_ref), (64, own_ref), (128 * odd, far_ref)):
        for half in range(2):
            for channel in range(4):
                value = acc_ref[4 * half + channel, pl.ds(pl.multiple_of(start, 64), 64), :]
                value = 1.0 - value if channel == 3 else value
                out_ref[pl.ds(64 * (4 * half + channel), 64), :] = value
    near_ref[pl.ds(512, 64), :] = rows_ref[pl.ds(pl.multiple_of(64 * odd, 64), 64), :]
    far_ref[pl.ds(512, 64), :] = rows_ref[pl.ds(pl.multiple_of(64 - 64 * odd, 64), 64), :]
    near_ref[pl.ds(576, 64), :] = cols_ref[...]
    far_ref[pl.ds(576, 64), :] = cols_ref[...]


def over(front, behind):
    through = 1.0 - front[3]
    return [front[c] + through * behind[c] for c in range(4)]


def channels(ref, *index):
    return [ref[(*index, c)] for c in range(4)]


def turn_rows(plane, amounts, share=1):
    sub = lax.broadcasted_iota(jnp.int32, (8, COLS), 0)
    tiles = []
    for t in range(plane.shape[0] // 8):
        tile = plane[8 * t : 8 * t + 8]
        turned = pltpu.roll(tile, amounts(8 * t // share), 1)
        for r in range(1, 8 // share):
            turned = jnp.where(sub // share == r, pltpu.roll(tile, amounts(8 * t // share + r), 1), turned)
        tiles.append(turned)
    return jnp.concatenate(tiles, axis=0)


def select_dot(chosen, values):
    coarse = values.astype(jnp.bfloat16)
    rest = (values - coarse.astype(jnp.float32)).astype(jnp.bfloat16)
    both = jnp.concatenate([coarse, rest], axis=0)
    return jnp.dot(chosen.astype(jnp.bfloat16), both, preferred_element_type=jnp.float32)


def line_composite(sheared, opticals, key_row, key_col):
    first = lax.broadcasted_iota(jnp.int32, (SLAB, 2 * SLAB), 0)
    second = lax.broadcasted_iota(jnp.int32, (SLAB, 2 * SLAB), 1) % SLAB
    ahead = jnp.where((second < first) & (key_row == key_col), 1.0, 0.0)
    target = lax.broadcasted_iota(jnp.int32, (2 * SLAB, 2 * SLAB), 0).astype(jnp.float32)
    chosen = jnp.where(target == key_row + 64.0, 1.0, 0.0)
    before = select_dot(ahead, jnp.concatenate(opticals, axis=1))
    tints = tint(sheared)
    pieces = []
    for half, optical in enumerate(opticals):
        front = before[:, COLS * half : COLS * half + COLS]
        weight = jnp.exp(-front) - jnp.exp(-(front + optical))
        pieces += [weight * tints[0], weight * tints[1], weight * tints[2], weight]
    total = select_dot(chosen, jnp.concatenate(pieces, axis=1))
    return [total[:, COLS * p : COLS * p + COLS] for p in range(len(pieces))]


def rows_kernel(
    scale, shift_ref, edge_ref, own_ref, near_ref, far_ref, rows_ref, cols_ref, fvec_ref, fcol_ref, fy_ref,
    mine_ref, near_out_ref, far_out_ref, u_ref,
):
    lane = lax.broadcasted_iota(jnp.int32, (1, COLS), 1)
    odd_row, odd_col = edge_ref[0] == 1, edge_ref[1] == 1
    fy, fx, rate = fcol_ref[:, 0:1], fcol_ref[:, 1:2], fcol_ref[:, 2:3] * scale
    oy, ox = fcol_ref[:, 3:4], fcol_ref[:, 4:5]

    def received(start, size):
        near, far = near_ref[pl.ds(start, size), :], far_ref[pl.ds(start, size), :]
        return jnp.where(odd_row, far, near), jnp.where(odd_row, near, far)

    below_row, above_row = received(512, 64)
    here = jnp.where(oy < 0.0, below_row, rows_ref[pl.ds(64, 64), :])
    behind = jnp.where(oy < 0.0, rows_ref[pl.ds(0, 64), :], above_row)
    mixed = here + fy * (behind - here)
    sheared = mixed + fx * (pltpu.roll(mixed, 1, 1) - mixed)
    sheared = turn_rows(sheared, lambda z: shift_ref[1, z] + 64)
    optical = rate * softplus(sheared)
    place = lane.astype(jnp.float32)
    opticals = [jnp.where(place > ox + 64.0, optical, 0.0), jnp.where(place < ox + 64.0, optical, 0.0)]
    line = line_composite(sheared, opticals, fvec_ref[6:7, :], oy)

    halves = []
    for half in range(2):
        pairs = [received(64 * (4 * half + c), 64) for c in range(4)]
        own = [own_ref[pl.ds(64 * (4 * half + c), 64), :] for c in range(4)]
        lower = [line[4 * half + c][:64] for c in range(4)]
        upper = [line[4 * half + c][64:] for c in range(4)]
        merged = over(own, over(upper, [above for _, above in pairs]))
        halves.append(over([below for below, _ in pairs], over(lower, merged)))
    for c in range(4):
        low, high = halves[0][c], halves[1][c]
        low_turned, high_turned = pltpu.roll(low, 64, 1), pltpu.roll(high, 64, 1)
        mine_ref[c] = jnp.where(lane < 64, low_turned, high_turned)
        left = jnp.where(lane < 64, low[:32], low_turned[32:])
        right = jnp.where(lane < 64, high_turned[:32], high[32:])
        near_out_ref[pl.ds(32 * c, 32), :] = jnp.where(odd_col, left, right)
        far_out_ref[pl.ds(32 * c, 32), :] = jnp.where(odd_col, right, left)

    below_col, above_col = received(576, 64)
    negative = fvec_ref[5:6, :] < 0.0
    pair = jnp.concatenate(
        [jnp.where(negative, cols_ref[...], above_col), jnp.where(negative, below_col, cols_ref[...])], axis=0
    )

    def amount(z):
        offset = shift_ref[0, z]
        return jnp.where(offset < 0, offset + COLS, offset + 64)

    here = turn_rows(jnp.transpose(pair), amount, 2)
    u_ref[...] = here + fy_ref[:, 0:1] * (pltpu.roll(here, 1, 1) - here)

    def pack(column):
        upper = u_ref[pl.ds(column, 32, stride=2), :]
        return jnp.where(lane < 64, upper, pltpu.roll(u_ref[pl.ds(64 + column, 32, stride=2), :], 64, 1))

    last, first = pack(0), pack(1)
    near_out_ref[pl.ds(128, 32), :] = jnp.where(odd_col, first, last)
    far_out_ref[pl.ds(128, 32), :] = jnp.where(odd_col, last, first)


def columns_kernel(scale, limit, edge_ref, mine_ref, near_ref, far_ref, u_ref, zrow_ref, zcol_ref, fvec_ref, fcol_ref, out_ref):
    lane = lax.broadcasted_iota(jnp.int32, (1, COLS), 1)
    odd_col = edge_ref[1] == 1
    fx, rate, oy, ox = fcol_ref[:, 1:2], fcol_ref[:, 2:3] * scale, fcol_ref[:, 3:4], fcol_ref[:, 4:5]

    def received(start, size):
        near, far = near_ref[pl.ds(start, size), :], far_ref[pl.ds(start, size), :]
        return jnp.where(odd_col, far, near), jnp.where(odd_col, near, far)

    right_first, left_last = [
        jnp.concatenate([part, pltpu.roll(part, 64, 1)], axis=0) for part in received(128, 32)
    ]
    here = jnp.where(ox < 0.0, right_first, u_ref[pl.ds(1, 64, stride=2), :])
    behind = jnp.where(ox < 0.0, u_ref[pl.ds(0, 64, stride=2), :], left_last)
    sheared = here + fx * (behind - here)
    row = (lane + edge_ref[2]).astype(jnp.float32) - oy
    optical = jnp.where((row >= 0.0) & (row <= limit), rate * softplus(sheared), 0.0)
    line = line_composite(sheared, [optical], fvec_ref[7:8, :], ox)
    line = [pltpu.roll(jnp.transpose(part)[:64], 64, 1) for part in line]

    front, behind = [], []
    for c in range(4):
        right, left = received(32 * c, 32)
        upper = jnp.concatenate([pltpu.roll(right, 64, 1), right], axis=0)
        lower = jnp.concatenate([left, pltpu.roll(left, 64, 1)], axis=0)
        own = mine_ref[c]
        front.append(jnp.where(lane < 64, own, upper))
        behind.append(jnp.where(lane < 64, lower, own))
    inner = over(front, over(line, behind))
    total = jnp.sum(fvec_ref[2:3, :], axis=1, keepdims=True)
    pre = jnp.maximum(zrow_ref[:, 0:1], zcol_ref[0:1, :])
    post = jnp.minimum(jnp.maximum(zrow_ref[:, 1:2], zcol_ref[1:2, :]), total - pre)
    flat = []
    for amount in (pre, jnp.maximum(post, 0.0)):
        fade = 1.0 - jnp.exp((-scale * LN2) * amount)
        flat.append([jnp.zeros_like(fade), fade, math.tanh(0.4) * fade, fade])
    whole = over(flat[0], over(inner, flat[1]))
    pieces = out_ref.shape[0]
    height = ROWS // pieces
    for p in range(pieces):
        for c in range(4):
            out_ref[p, c] = whole[c][p * height : (p + 1) * height]


def fold_kernel(in_ref, out_ref):
    merged = channels(in_ref, 0)
    for slab in range(1, in_ref.shape[0]):
        merged = over(merged, channels(in_ref, slab))
    out_ref[0] = 0.5 * (merged[3] + merged[0])
    out_ref[1] = merged[1]
    out_ref[2] = 0.5 * (merged[3] + merged[2])
    out_ref[3] = merged[3]


def tile_scratch():
    return [
        pltpu.SMEM((2, SLAB), jnp.int32),
        pltpu.SMEM((2, SLAB), jnp.float32),
        pltpu.SMEM((SLAB,), jnp.float32),
        pltpu.VMEM((SLAB, ROWS, COLS), jnp.float32),
        pltpu.VMEM((16, 16, COLS), jnp.float32),
        pltpu.VMEM((32, 32, COLS), jnp.float32),
        pltpu.VMEM((64, 64, COLS), jnp.float32),
        pltpu.VMEM((64, COLS), jnp.float32),
        pltpu.VMEM((8, EXT, COLS), jnp.float32),
        pltpu.SemaphoreType.DMA((10,)),
    ]


def matching(count, first):
    pairs = [(i, i + 1) for i in range(first, count - 1, 2)]
    return pairs + [(j, i) for i, j in pairs]


def body(coefficients, shifts, fraction, absorb):
    depth_count = lax.axis_size("depth")
    row_count = lax.axis_size("imgy")
    col_count = lax.axis_size("imgx")
    scale = 2.0 / (SLAB * depth_count)
    iy, ix = lax.axis_index("imgy"), lax.axis_index("imgx")

    shift_rows, shift_cols = shifts[0], shifts[1]
    edge = jnp.stack([iy % 2, ix % 2, iy * ROWS]).astype(jnp.int32)
    lines = jnp.concatenate([fraction, absorb[None], shifts.astype(jnp.float32)], axis=0)
    twice = jnp.repeat(lines[3:4], 2, axis=1)
    tiled = jnp.tile(lines[3:5], (1, 2))
    vectors = jnp.concatenate([jnp.pad(lines, ((0, 0), (0, COLS - SLAB))), twice, tiled], axis=0)
    fy_twice = jnp.repeat(fraction[0], 2)[:, None]
    columns = jnp.pad(lines.T, ((0, 0), (0, 3)))

    sent = f32(640, COLS)
    near, own, far, row_planes, col_planes = call(
        functools.partial(tile_kernel, scale),
        (sent, f32(512, COLS), sent, f32(128, COLS), f32(64, COLS)),
        [SMEM_SPEC] + [HBM_SPEC] * 4,
        tile_scratch(),
        flops=300_000_000,
        bytes_moved=4 << 20,
    )(edge, *[pltpu.with_memory_space_constraint(a, pltpu.HBM) for a in (shifts, fraction, absorb, coefficients)])

    far = lax.ppermute(far, "imgy", matching(row_count, 1))
    near = lax.ppermute(near, "imgy", matching(row_count, 0))
    packed = f32(160, COLS)
    mine, near, far, sheared_cols = call(
        functools.partial(rows_kernel, scale),
        (f32(4, ROWS, COLS), packed, packed, f32(128, COLS)),
        [SMEM_SPEC] * 2 + [VMEM_SPEC] * 8,
    )(shifts, edge, own, near, far, row_planes, col_planes, vectors, columns, fy_twice)
    far = lax.ppermute(far, "imgx", matching(col_count, 1))
    near = lax.ppermute(near, "imgx", matching(col_count, 0))

    image_rows = iy * ROWS + jnp.arange(ROWS, dtype=jnp.int32)
    image_cols = ix * COLS + jnp.arange(COLS, dtype=jnp.int32)

    def outside(pixels, offsets, limit):
        position = pixels[:, None] - offsets[None, :]
        pre = jnp.sum(jnp.where(position > limit, absorb[None, :], 0.0), axis=1)
        post = jnp.sum(jnp.where(position < 0, absorb[None, :], 0.0), axis=1)
        return pre, post

    zrow = jnp.stack(outside(image_rows, shift_rows, ROWS * row_count), axis=1)
    zcol = jnp.stack(outside(image_cols, shift_cols, COLS * col_count), axis=0)
    pieces = call(
        functools.partial(columns_kernel, scale, float(ROWS * row_count)),
        f32(depth_count, 4, ROWS // depth_count, COLS),
        [SMEM_SPEC] + [VMEM_SPEC] * 8,
    )(edge, mine, near, far, sheared_cols, zrow, zcol, vectors, columns)
    incoming = lax.all_to_all(pieces, "depth", split_axis=0, concat_axis=0, tiled=True)
    image = call(fold_kernel, f32(4, ROWS // depth_count, COLS), [VMEM_SPEC])(incoming)
    return image[:, None]


def solution(mesh):
    in_specs = (P("depth", "imgy", "imgx"), P(None, "depth"), P(None, "depth"), P("depth"))
    out_specs = P(None, "imgy", "depth", "imgx")
    return jax.shard_map(body, mesh=mesh, in_specs=in_specs, out_specs=out_specs, check_vma=False)
```

```python
import functools
import math

import jax
import jax.numpy as jnp
from jax import lax
from jax.experimental import pallas as pl
from jax.experimental.pallas import tpu as pltpu
from jax.sharding import PartitionSpec as P


BRICK = 64
SLAB = 64
ROWS = 64
COLS = 128
EXT = 208
SLICE_UNROLL = 16
LN2 = math.log(2.0)
LOG2E = 1.0 / math.log(2.0)
VMEM_SPEC = pl.BlockSpec(memory_space=pltpu.VMEM)
SMEM_SPEC = pl.BlockSpec(memory_space=pltpu.SMEM)
HBM_SPEC = pl.BlockSpec(memory_space=pltpu.HBM)
INTERPRET = False


def call(kernel, out_shape, in_specs, scratch=(), flops=1000, bytes_moved=1000):
    specs = jax.tree.map(lambda _: VMEM_SPEC, out_shape)
    return pl.pallas_call(
        kernel,
        out_shape=out_shape,
        in_specs=in_specs,
        out_specs=specs,
        scratch_shapes=list(scratch),
        interpret=INTERPRET,
        compiler_params=pltpu.CompilerParams(vmem_limit_bytes=24 << 20),
        cost_estimate=pl.CostEstimate(flops=flops, bytes_accessed=bytes_moved, transcendentals=0),
    )


def f32(*shape):
    return jax.ShapeDtypeStruct(shape, jnp.float32)


def lane_table(half):
    source = lax.broadcasted_iota(jnp.int32, (2 * COLS, COLS), 0) % COLS
    target = lax.broadcasted_iota(jnp.int32, (2 * COLS, COLS), 1)
    local = target % BRICK
    start = target - local
    pair = local // 2
    weight = jnp.where(local % 2 == 1, 0.5, -0.5)
    inside = local < 2 * half
    low = jnp.where(inside & (source == start + pair), 1.0, 0.0)
    high = jnp.where(inside & (source == start + half + pair), weight, 0.0)
    return (low + high).astype(jnp.bfloat16)


def lane_lift(block, table):
    coarse = block.astype(jnp.bfloat16)
    rest = (block - coarse.astype(jnp.float32)).astype(jnp.bfloat16)
    both = jnp.concatenate([coarse, rest], axis=1)
    return jnp.dot(both, table, preferred_element_type=jnp.float32)


def softplus(sheared):
    return jnp.maximum(sheared, 0.0) + jnp.log(1.0 + jnp.exp(-jnp.abs(sheared)))


def tint(sheared):
    return jnp.tanh(0.75 * sheared), jnp.exp(-0.5 * (sheared * sheared)), jnp.tanh(0.4 - 0.5 * sheared)


def tile_kernel(
    scale, edge_ref, shift_hbm, frac_hbm, absorb_hbm, c_hbm, near_ref, acc_ref, far_ref, rows_ref, cols_ref,
    shift_ref, frac_ref, absorb_ref, c_ref, s2_ref, s1_ref, d_ref, plane_ref, sems,
):
    def load(index, planes, rows):
        block = (pl.ds(*planes), pl.ds(*rows))
        return pltpu.make_async_copy(c_hbm.at[block], c_ref.at[block], sems.at[index])

    loads = [load(0, (0, 16), (0, 16)), load(1, (16, 16), (0, 32)), load(2, (0, 16), (16, 16))]
    loads += [load(3, (0, 16), (32, 32)), load(4, (32, 16), (0, 64)), load(5, (16, 16), (32, 32)), load(6, (48, 16), (0, 64))]
    scalars = [
        pltpu.make_async_copy(shift_hbm, shift_ref, sems.at[7]),
        pltpu.make_async_copy(frac_hbm, frac_ref, sems.at[8]),
        pltpu.make_async_copy(absorb_hbm, absorb_ref, sems.at[9]),
    ]
    for copy in loads + scalars:
        copy.start()
    for index in range(8):
        acc_ref[index] = jnp.full((EXT, COLS), 1.0 if index % 4 == 3 else 0.0, jnp.float32)

    lane = lax.broadcasted_iota(jnp.int32, (1, COLS), 1)
    sub = lax.broadcasted_iota(jnp.int32, (8, COLS), 0)

    tables = {half: lane_table(half) for half in (8, 16, 32)}

    def level(half, below, out_ref, on_result, init, unroll, span=None):
        table = tables[half]

        def step(i, carry):
            if below is None:
                low = c_ref[i, : 2 * half, :]
            else:
                corner = jnp.where(lane % BRICK < half, below[i], c_ref[i, :half, :])
                low = jnp.concatenate([corner, c_ref[i, half : 2 * half, :]], axis=0)
            high = c_ref[i + half, : 2 * half, :]
            planes = []
            even = low - 0.5 * high
            for part in (even, even + high):
                row_even = part[:half] - 0.5 * part[half:]
                planes += [row_even, row_even + part[half:]]
            result = lane_lift(jnp.concatenate(planes, axis=0), table)
            for odd in range(2):
                for row_odd in range(2):
                    start = (2 * odd + row_odd) * half
                    out_ref[2 * i + odd, pl.ds(row_odd, half, stride=2), :] = result[start : start + half]
            return on_result(i, result, carry)

        first, last = span or (0, half)
        return lax.fori_loop(first, last, step, init, unroll=unroll)

    def ignore(i, result, carry):
        return carry

    def boundary(i, result, plane):
        for odd in range(2):
            z = 2 * i + odd
            piece = result[64 * odd : 64 * odd + 64]
            rows_ref[pl.ds(z, 1), :] = piece[63:64]
            rows_ref[pl.ds(64 + z, 1), :] = piece[0:1]
            plane = jnp.where(lane // 2 == z, pltpu.roll(piece, 2 * z + 1, 1), plane)
        return plane

    loads[0].wait()
    level(8, None, s2_ref, ignore, 0, 8)
    loads[1].wait()
    loads[2].wait()
    level(16, s2_ref, s1_ref, ignore, 0, 16)
    loads[3].wait()
    loads[4].wait()
    plane = level(32, s1_ref, d_ref, boundary, jnp.zeros((64, COLS), jnp.float32), 16, (0, 16))
    loads[5].wait()
    loads[6].wait()
    plane_ref[...] = level(32, s1_ref, d_ref, boundary, plane, 16, (16, 32))
    for row_odd in range(2):
        cols_ref[pl.ds(row_odd, 32, stride=2), :] = plane_ref[pl.ds(32 * row_odd, 32), :]

    for copy in scalars:
        copy.wait()

    inside = lax.broadcasted_iota(jnp.int32, (ROWS, COLS), 0) > 0

    def slice_step(z, carry):
        k = shift_ref[1, z] + 64
        here = d_ref[z]
        behind = jnp.concatenate([pltpu.roll(d_ref[z, 0:8, :], 1, 0), d_ref[z, 7:63, :]], axis=0)
        mixed = here + frac_ref[0, z] * (behind - here)
        left = pltpu.roll(mixed, 1, 1)
        sheared = pltpu.roll(mixed + frac_ref[1, z] * (left - mixed), k, 1)
        twos = LOG2E * sheared
        positive = jnp.maximum(twos, 0.0)
        soft = positive + jnp.log2(1.0 + jnp.exp2((twos - positive) - positive))
        keep = jnp.exp2((-absorb_ref[z] * scale) * soft)
        tints = jnp.tanh(0.75 * sheared), jnp.exp2((-0.5 * twos) * sheared), jnp.tanh(0.4 - 0.5 * sheared)
        view = acc_ref.at[:, pl.ds(shift_ref[0, z] + 64, 64), :]
        right = lane < k
        value = [jnp.where(right, view[4 + c], view[c]) for c in range(4)]
        after = value[3] * keep
        weight = value[3] - after
        value = [value[c] + weight * tints[c] for c in range(3)] + [after]
        for c in range(4):
            pltpu.store(view.at[c], value[c], mask=inside & (lane > k))
            pltpu.store(view.at[4 + c], value[c], mask=inside & right)
        return carry

    lax.fori_loop(0, SLAB, slice_step, 0, unroll=SLICE_UNROLL)

    odd = edge_ref[0]
    for start, out_ref in ((128 - 128 * odd, near_ref), (128 * odd, far_ref)):
        for half in range(2):
            for channel in range(4):
                value = acc_ref[4 * half + channel, pl.ds(pl.multiple_of(start, 64), 64), :]
                value = 1.0 - value if channel == 3 else value
                out_ref[pl.ds(64 * (4 * half + channel), 64), :] = value
    near_ref[pl.ds(512, 64), :] = rows_ref[pl.ds(pl.multiple_of(64 * odd, 64), 64), :]
    far_ref[pl.ds(512, 64), :] = rows_ref[pl.ds(pl.multiple_of(64 - 64 * odd, 64), 64), :]
    near_ref[pl.ds(576, 64), :] = cols_ref[...]
    far_ref[pl.ds(576, 64), :] = cols_ref[...]


def over(front, behind):
    through = 1.0 - front[3]
    return [front[c] + through * behind[c] for c in range(4)]


def channels(ref, *index):
    return [ref[(*index, c)] for c in range(4)]


def turn_rows(plane, amounts, share=1):
    sub = lax.broadcasted_iota(jnp.int32, (8, COLS), 0)
    tiles = []
    for t in range(plane.shape[0] // 8):
        tile = plane[8 * t : 8 * t + 8]
        turned = pltpu.roll(tile, amounts(8 * t // share), 1)
        for r in range(1, 8 // share):
            turned = jnp.where(sub // share == r, pltpu.roll(tile, amounts(8 * t // share + r), 1), turned)
        tiles.append(turned)
    return jnp.concatenate(tiles, axis=0)


def select_dot(chosen, values):
    coarse = values.astype(jnp.bfloat16)
    rest = (values - coarse.astype(jnp.float32)).astype(jnp.bfloat16)
    both = jnp.concatenate([coarse, rest], axis=0)
    return jnp.dot(chosen.astype(jnp.bfloat16), both, preferred_element_type=jnp.float32)


def line_composite(sheared, opticals, key_row, key_col):
    first = lax.broadcasted_iota(jnp.int32, (SLAB, 2 * SLAB), 0)
    second = lax.broadcasted_iota(jnp.int32, (SLAB, 2 * SLAB), 1) % SLAB
    ahead = jnp.where((second < first) & (key_row == key_col), 1.0, 0.0)
    target = lax.broadcasted_iota(jnp.int32, (2 * SLAB, 2 * SLAB), 0).astype(jnp.float32)
    chosen = jnp.where(target == key_row + 64.0, 1.0, 0.0)
    before = select_dot(ahead, jnp.concatenate(opticals, axis=1))
    tints = tint(sheared)
    pieces = []
    for half, optical in enumerate(opticals):
        front = before[:, COLS * half : COLS * half + COLS]
        weight = jnp.exp(-front) - jnp.exp(-(front + optical))
        pieces += [weight * tints[0], weight * tints[1], weight * tints[2], weight]
    total = select_dot(chosen, jnp.concatenate(pieces, axis=1))
    return [total[:, COLS * p : COLS * p + COLS] for p in range(len(pieces))]


def rows_kernel(
    scale, shift_ref, edge_ref, own_ref, near_ref, far_ref, rows_ref, cols_ref, fvec_ref, fcol_ref, fy_ref,
    mine_ref, near_out_ref, far_out_ref, u_ref,
):
    lane = lax.broadcasted_iota(jnp.int32, (1, COLS), 1)
    odd_row, odd_col = edge_ref[0] == 1, edge_ref[1] == 1
    fy, fx, rate = fcol_ref[:, 0:1], fcol_ref[:, 1:2], fcol_ref[:, 2:3] * scale
    oy, ox = fcol_ref[:, 3:4], fcol_ref[:, 4:5]

    def received(start, size):
        near, far = near_ref[pl.ds(start, size), :], far_ref[pl.ds(start, size), :]
        return jnp.where(odd_row, far, near), jnp.where(odd_row, near, far)

    below_row, above_row = received(512, 64)
    here = jnp.where(oy < 0.0, below_row, rows_ref[pl.ds(64, 64), :])
    behind = jnp.where(oy < 0.0, rows_ref[pl.ds(0, 64), :], above_row)
    mixed = here + fy * (behind - here)
    sheared = mixed + fx * (pltpu.roll(mixed, 1, 1) - mixed)
    sheared = turn_rows(sheared, lambda z: shift_ref[1, z] + 64)
    optical = rate * softplus(sheared)
    place = lane.astype(jnp.float32)
    opticals = [jnp.where(place > ox + 64.0, optical, 0.0), jnp.where(place < ox + 64.0, optical, 0.0)]
    line = line_composite(sheared, opticals, fvec_ref[6:7, :], oy)

    halves = []
    for half in range(2):
        pairs = [received(64 * (4 * half + c), 64) for c in range(4)]
        own = [own_ref[4 * half + c, pl.ds(64, 64), :] for c in range(4)]
        own[3] = 1.0 - own[3]
        lower = [line[4 * half + c][:64] for c in range(4)]
        upper = [line[4 * half + c][64:] for c in range(4)]
        merged = over(own, over(upper, [above for _, above in pairs]))
        halves.append(over([below for below, _ in pairs], over(lower, merged)))
    for c in range(4):
        low, high = halves[0][c], halves[1][c]
        low_turned, high_turned = pltpu.roll(low, 64, 1), pltpu.roll(high, 64, 1)
        mine_ref[c] = jnp.where(lane < 64, low_turned, high_turned)
        left = jnp.where(lane < 64, low[:32], low_turned[32:])
        right = jnp.where(lane < 64, high_turned[:32], high[32:])
        near_out_ref[pl.ds(32 * c, 32), :] = jnp.where(odd_col, left, right)
        far_out_ref[pl.ds(32 * c, 32), :] = jnp.where(odd_col, right, left)

    below_col, above_col = received(576, 64)
    negative = fvec_ref[5:6, :] < 0.0
    pair = jnp.concatenate(
        [jnp.where(negative, cols_ref[...], above_col), jnp.where(negative, below_col, cols_ref[...])], axis=0
    )

    def amount(z):
        offset = shift_ref[0, z]
        return jnp.where(offset < 0, offset + COLS, offset + 64)

    here = turn_rows(jnp.transpose(pair), amount, 2)
    u_ref[...] = here + fy_ref[:, 0:1] * (pltpu.roll(here, 1, 1) - here)

    def pack(column):
        upper = u_ref[pl.ds(column, 32, stride=2), :]
        return jnp.where(lane < 64, upper, pltpu.roll(u_ref[pl.ds(64 + column, 32, stride=2), :], 64, 1))

    last, first = pack(0), pack(1)
    near_out_ref[pl.ds(128, 32), :] = jnp.where(odd_col, first, last)
    far_out_ref[pl.ds(128, 32), :] = jnp.where(odd_col, last, first)


def columns_kernel(scale, limit, edge_ref, mine_ref, near_ref, far_ref, u_ref, zrow_ref, zcol_ref, fvec_ref, fcol_ref, out_ref):
    lane = lax.broadcasted_iota(jnp.int32, (1, COLS), 1)
    odd_col = edge_ref[1] == 1
    fx, rate, oy, ox = fcol_ref[:, 1:2], fcol_ref[:, 2:3] * scale, fcol_ref[:, 3:4], fcol_ref[:, 4:5]

    def received(start, size):
        near, far = near_ref[pl.ds(start, size), :], far_ref[pl.ds(start, size), :]
        return jnp.where(odd_col, far, near), jnp.where(odd_col, near, far)

    right_first, left_last = [
        jnp.concatenate([part, pltpu.roll(part, 64, 1)], axis=0) for part in received(128, 32)
    ]
    here = jnp.where(ox < 0.0, right_first, u_ref[pl.ds(1, 64, stride=2), :])
    behind = jnp.where(ox < 0.0, u_ref[pl.ds(0, 64, stride=2), :], left_last)
    sheared = here + fx * (behind - here)
    row = (lane + edge_ref[2]).astype(jnp.float32) - oy
    optical = jnp.where((row >= 0.0) & (row <= limit), rate * softplus(sheared), 0.0)
    line = line_composite(sheared, [optical], fvec_ref[7:8, :], ox)
    line = [pltpu.roll(jnp.transpose(part)[:64], 64, 1) for part in line]

    front, behind = [], []
    for c in range(4):
        right, left = received(32 * c, 32)
        upper = jnp.concatenate([pltpu.roll(right, 64, 1), right], axis=0)
        lower = jnp.concatenate([left, pltpu.roll(left, 64, 1)], axis=0)
        own = mine_ref[c]
        front.append(jnp.where(lane < 64, own, upper))
        behind.append(jnp.where(lane < 64, lower, own))
    inner = over(front, over(line, behind))
    total = jnp.sum(fvec_ref[2:3, :], axis=1, keepdims=True)
    pre = jnp.maximum(zrow_ref[:, 0:1], zcol_ref[0:1, :])
    post = jnp.minimum(jnp.maximum(zrow_ref[:, 1:2], zcol_ref[1:2, :]), total - pre)
    flat = []
    for amount in (pre, jnp.maximum(post, 0.0)):
        fade = 1.0 - jnp.exp((-scale * LN2) * amount)
        flat.append([jnp.zeros_like(fade), fade, math.tanh(0.4) * fade, fade])
    whole = over(flat[0], over(inner, flat[1]))
    pieces = out_ref.shape[0]
    height = ROWS // pieces
    for p in range(pieces):
        for c in range(4):
            out_ref[p, c] = whole[c][p * height : (p + 1) * height]


def fold_kernel(in_ref, out_ref):
    merged = channels(in_ref, 0)
    for slab in range(1, in_ref.shape[0]):
        merged = over(merged, channels(in_ref, slab))
    out_ref[0] = 0.5 * (merged[3] + merged[0])
    out_ref[1] = merged[1]
    out_ref[2] = 0.5 * (merged[3] + merged[2])
    out_ref[3] = merged[3]


def tile_scratch():
    return [
        pltpu.SMEM((2, SLAB), jnp.int32),
        pltpu.SMEM((2, SLAB), jnp.float32),
        pltpu.SMEM((SLAB,), jnp.float32),
        pltpu.VMEM((SLAB, ROWS, COLS), jnp.float32),
        pltpu.VMEM((16, 16, COLS), jnp.float32),
        pltpu.VMEM((32, 32, COLS), jnp.float32),
        pltpu.VMEM((64, 64, COLS), jnp.float32),
        pltpu.VMEM((64, COLS), jnp.float32),
        pltpu.SemaphoreType.DMA((10,)),
    ]


def matching(count, first):
    pairs = [(i, i + 1) for i in range(first, count - 1, 2)]
    return pairs + [(j, i) for i, j in pairs]


def body(coefficients, shifts, fraction, absorb):
    depth_count = lax.axis_size("depth")
    row_count = lax.axis_size("imgy")
    col_count = lax.axis_size("imgx")
    scale = 2.0 / (SLAB * depth_count)
    iy, ix = lax.axis_index("imgy"), lax.axis_index("imgx")

    shift_rows, shift_cols = shifts[0], shifts[1]
    edge = jnp.stack([iy % 2, ix % 2, iy * ROWS]).astype(jnp.int32)
    lines = jnp.concatenate([fraction, absorb[None], shifts.astype(jnp.float32)], axis=0)
    twice = jnp.repeat(lines[3:4], 2, axis=1)
    tiled = jnp.tile(lines[3:5], (1, 2))
    vectors = jnp.concatenate([jnp.pad(lines, ((0, 0), (0, COLS - SLAB))), twice, tiled], axis=0)
    fy_twice = jnp.repeat(fraction[0], 2)[:, None]
    columns = jnp.pad(lines.T, ((0, 0), (0, 3)))

    sent = f32(640, COLS)
    near, own, far, row_planes, col_planes = call(
        functools.partial(tile_kernel, scale),
        (sent, f32(8, EXT, COLS), sent, f32(128, COLS), f32(64, COLS)),
        [SMEM_SPEC] + [HBM_SPEC] * 4,
        tile_scratch(),
        flops=300_000_000,
        bytes_moved=4 << 20,
    )(edge, *[pltpu.with_memory_space_constraint(a, pltpu.HBM) for a in (shifts, fraction, absorb, coefficients)])

    far = lax.ppermute(far, "imgy", matching(row_count, 1))
    near = lax.ppermute(near, "imgy", matching(row_count, 0))
    packed = f32(160, COLS)
    mine, near, far, sheared_cols = call(
        functools.partial(rows_kernel, scale),
        (f32(4, ROWS, COLS), packed, packed, f32(128, COLS)),
        [SMEM_SPEC] * 2 + [VMEM_SPEC] * 8,
    )(shifts, edge, own, near, far, row_planes, col_planes, vectors, columns, fy_twice)
    far = lax.ppermute(far, "imgx", matching(col_count, 1))
    near = lax.ppermute(near, "imgx", matching(col_count, 0))

    image_rows = iy * ROWS + jnp.arange(ROWS, dtype=jnp.int32)
    image_cols = ix * COLS + jnp.arange(COLS, dtype=jnp.int32)

    def outside(pixels, offsets, limit):
        position = pixels[:, None] - offsets[None, :]
        pre = jnp.sum(jnp.where(position > limit, absorb[None, :], 0.0), axis=1)
        post = jnp.sum(jnp.where(position < 0, absorb[None, :], 0.0), axis=1)
        return pre, post

    zrow = jnp.stack(outside(image_rows, shift_rows, ROWS * row_count), axis=1)
    zcol = jnp.stack(outside(image_cols, shift_cols, COLS * col_count), axis=0)
    pieces = call(
        functools.partial(columns_kernel, scale, float(ROWS * row_count)),
        f32(depth_count, 4, ROWS // depth_count, COLS),
        [SMEM_SPEC] + [VMEM_SPEC] * 8,
    )(edge, mine, near, far, sheared_cols, zrow, zcol, vectors, columns)
    incoming = lax.all_to_all(pieces, "depth", split_axis=0, concat_axis=0, tiled=True)
    image = call(fold_kernel, f32(4, ROWS // depth_count, COLS), [VMEM_SPEC])(incoming)
    return image[:, None]


def solution(mesh):
    in_specs = (P("depth", "imgy", "imgx"), P(None, "depth"), P(None, "depth"), P("depth"))
    out_specs = P(None, "imgy", "depth", "imgx")
    return jax.shard_map(body, mesh=mesh, in_specs=in_specs, out_specs=out_specs, check_vma=False)
```
